512 devices in a mesh: space: 64 (over x, y, z_lo), dp: 8 (over z_hi, core).
Axes of the slice: x: 4, y: 8, z: 8 (z_hi: 4, z_lo: 2; z = z_hi * 2 + z_lo), core: 2. Of those that a mesh axis runs over, the one named last changes fastest.
Arguments:
- volumes: bfloat16 [8, 4, 256, 32, 32], P('dp', None, 'space'), may hold values from -6 to 6
- kernel_one: bfloat16 [32, 4, 3, 3, 3], replicated, may hold values from -0.625 to 0.625
- kernel_two: bfloat16 [64, 32, 3, 3, 3], replicated, may hold values from -0.21875 to 0.21875
- cotangent: bfloat16 [8, 64, 128, 256], P('dp', None, 'space'), may hold values from -6 to 6
Outputs:
- features: bfloat16 [8, 64, 128, 256], P('dp', None, 'space')
- pooled_grad: bfloat16 [8, 32, 128, 256], P('dp', None, 'space')
- grad_one: float32 [3456], P('space')
- grad_two: float32 [55296], P('space')
The draws below stay inside these ranges and needn't reach their ends.
All inputs are finite; a program needn't handle non-finite values.
Results may differ from the reference program's by a relative error of at most 0.006.
Values may be sent and summed in bfloat16 or wider, within the bound.
A program may use at most 64 MiB of HBM per device.

```python
import jax
import jax.numpy as jnp
from jax import lax

CIN = 4
C1 = 32
C2 = 64
W = 32
VOLS = 8
NX = 256


def level_of(rng, extent, split, least, largest):
    loudness = 1.0
    for dim, blocks in split:
        draws = jax.random.uniform(jax.random.fold_in(jax.random.fold_in(rng, 6), dim), (blocks,), jnp.float32, least / len(split), largest / len(split))
        loudness = loudness * jnp.repeat(jnp.exp(draws), extent[dim] // blocks).reshape((-1,) + (1,) * (len(extent) - 1 - dim))
    return loudness


def centred(stream_key, shape, width, limit, cuts=(), dtype=jnp.bfloat16):
    loudness = level_of(stream_key, shape, cuts, -0.22, 0.18) if cuts else 1.0
    array = jax.random.normal(stream_key, shape, jnp.float32) * width * loudness
    return jnp.minimum(jnp.maximum(array, -limit), limit).astype(dtype)


def setup_inputs(seed: int = 0) -> dict:
    key_list = jax.random.split(jax.random.key(seed), 5)
    volumes = centred(key_list[0], (VOLS, CIN, NX, W, W), 1.0, 6.0, ((0, 8), (2, 64)))
    kernel_one = centred(key_list[1], (C1, CIN, 3, 3, 3), (CIN * 27) ** -0.5, 0.625)
    kernel_two = centred(key_list[2], (C2, C1, 3, 3, 3), (C1 * 27) ** -0.5, 0.21875)
    cotangent = centred(key_list[3], (VOLS, C2, NX // 2, (W // 2) * (W // 2)), 1.0, 6.0, ((0, 8), (2, 64)))
    return dict(volumes=volumes, kernel_one=kernel_one, kernel_two=kernel_two, cotangent=cotangent)


def silu(v):
    return v * jax.nn.sigmoid(v)

def dsilu(v):
    s = jax.nn.sigmoid(v)
    return s * (1.0 + v * (1.0 - s))

def conv_same(inputs, kernel):
    return lax.conv_general_dilated(inputs[None], kernel, (1, 1, 1), [(1, 1), (1, 1), (1, 1)], dimension_numbers=('NCDHW', 'OIDHW', 'NCDHW'), precision=lax.Precision.HIGHEST)[0]

def kernel_grad(inputs, delta):
    padded = jnp.pad(inputs, ((0, 0), (1, 1), (1, 1), (1, 1)))
    result = lax.conv_general_dilated(padded[:, None], delta[:, None], (1, 1, 1), 'VALID', dimension_numbers=('NCDHW', 'OIDHW', 'NCDHW'), precision=lax.Precision.HIGHEST)
    return jnp.transpose(result, (1, 0, 2, 3, 4))

def pool_cells(field):
    chans, depth, rows, cols = field.shape
    return field.reshape(chans, depth // 2, 2, rows // 2, 2, cols // 2, 2).mean(axis=(2, 4, 6))

def spread_cells(field):
    return jnp.repeat(jnp.repeat(jnp.repeat(field, 2, axis=1), 2, axis=2), 2, axis=3) * 0.125

def reference(volumes, kernel_one, kernel_two, cotangent):
    first = kernel_one.astype(jnp.float32)
    second = kernel_two.astype(jnp.float32)
    flipped = jnp.transpose(jnp.flip(second, (2, 3, 4)), (1, 0, 2, 3, 4))
    half = W // 2

    def one_volume(pair):
        volume, cot_flat = pair
        cot = cot_flat.reshape(cot_flat.shape[0], cot_flat.shape[1], half, half)
        inputs = volume.astype(jnp.float32)
        pre_one = conv_same(inputs, first)
        pooled = pool_cells(silu(pre_one)).astype(jnp.bfloat16)
        pooled_f = lax.optimization_barrier(pooled).astype(jnp.float32)
        pre_two = conv_same(pooled_f, second)
        feats = silu(pre_two).astype(jnp.bfloat16)
        delta_two = (cot.astype(jnp.float32) * dsilu(pre_two)).astype(jnp.bfloat16)
        delta_two_f = lax.optimization_barrier(delta_two).astype(jnp.float32)
        pgrad = conv_same(delta_two_f, flipped).astype(jnp.bfloat16)
        pgrad_f = lax.optimization_barrier(pgrad).astype(jnp.float32)
        delta_one = (spread_cells(pgrad_f) * dsilu(pre_one)).astype(jnp.bfloat16)
        delta_one_f = lax.optimization_barrier(delta_one).astype(jnp.float32)
        term_one = kernel_grad(inputs, delta_one_f)
        term_two = kernel_grad(pooled_f, delta_two_f)
        feats_flat = feats.reshape(feats.shape[0], feats.shape[1], half * half)
        pgrad_flat = pgrad.reshape(pgrad.shape[0], pgrad.shape[1], half * half)
        return (feats_flat, pgrad_flat, term_one, term_two)
    feats, pgrad, terms_one, terms_two = lax.map(one_volume, (volumes, cotangent))
    count = VOLS * NX * W * W
    grad_one = lax.optimization_barrier(jnp.sum(terms_one, axis=0)) / jnp.sqrt(jnp.float32(count))
    grad_two = lax.optimization_barrier(jnp.sum(terms_two, axis=0)) / jnp.sqrt(jnp.float32(count // 8))
    return (feats, pgrad, grad_one.reshape(-1), grad_two.reshape(-1))
```

```python
import functools
import math

import jax
import jax.numpy as jnp
from jax import lax
from jax.experimental import pallas as pl
from jax.experimental.pallas import tpu as pltpu
from jax.sharding import PartitionSpec as P

F32 = jnp.float32
BF16 = jnp.bfloat16
TAPS = [(a, b) for a in (-1, 0, 1) for b in (-1, 0, 1)]
NT = (((1,), (1,)), ((), ()))


def dot(a, b):
    return jnp.dot(a, b, preferred_element_type=F32)


def dot_nt(a, b):
    return lax.dot_general(a, b, NT, preferred_element_type=F32)


def iota(shape, dim):
    return lax.broadcasted_iota(jnp.int32, shape, dim)


def tap_masks(width):
    lane = iota((1, width * width), 1)
    row, col = lane // width, lane % width
    rows = {-1: row >= 1, 0: None, 1: row < width - 1}
    cols = {-1: col >= 1, 0: None, 1: col < width - 1}
    masks = []
    for dr, dc in TAPS:
        parts = [m for m in (rows[dr], cols[dc]) if m is not None]
        mask = None
        for part in parts:
            mask = part if mask is None else jnp.logical_and(mask, part)
        masks.append(mask)
    return masks


def shifted(block, tap, masks, width, sign=1):
    dr, dc = TAPS[tap]
    dr, dc = sign * dr, sign * dc
    if dr == 0 and dc == 0:
        return block
    size = width * width
    moved = pltpu.roll(block, (-(dr * width + dc)) % size, 1)
    return jnp.where(masks[TAPS.index((dr, dc))], moved, 0.0)


def sigmoid(v):
    return 1.0 / (1.0 + jnp.exp(-v))


def kernel(
    sizes,
    vol, w1, w2, cot,
    feat, pgrad, g1_out, g2_out,
    h1, x1, tsel, w1big, pool, dsilu_one, w2band, wp, cotf,
    pext, xcol, dext,
    g2f, g2s, g2x, g2yf, g2ys, g2y, g2z, g2r,
    g1s, g1x, g1ys, g1y, g1z, g1r,
    halo_send, halo_recv, xs, xr, ys, yr, zs, zr,
):
    nx, ny, nz, dp_n = sizes
    slabs = nx * ny * nz
    space = lax.axis_index("space")
    dp = lax.axis_index("dp")
    zl = lax.rem(space, nz)
    xy = lax.div(space, nz)
    yi = lax.rem(xy, ny)
    xi = lax.div(xy, ny)
    nxt = lax.rem(space + 1, slabs)
    prv = lax.rem(space + slabs - 1, slabs)
    team = nz * dp_n
    me_z = zl * dp_n + dp

    def x_peer(r):
        other = lax.rem(xi + r, nx)
        return other, ((other * ny + yi) * nz + zl, dp)

    def y_peer(r):
        other = lax.rem(yi + r, ny)
        return other, ((xi * ny + other) * nz + zl, dp)

    def z_peer(r):
        other = lax.rem(me_z + r, team)
        oz = lax.div(other, dp_n)
        return other, oz, (xy * nz + oz, lax.rem(other, dp_n))

    barrier = pltpu.get_barrier_semaphore()
    peers = [(nxt, dp), (prv, dp)]
    peers += [x_peer(r)[1] for r in range(1, nx)]
    peers += [y_peer(r)[1] for r in range(1, ny)]
    peers += [z_peer(r)[2] for r in range(1, team)]
    for peer in peers:
        pl.semaphore_signal(barrier, inc=1, device_id=peer, device_id_type=pl.DeviceIdType.MESH)

    def send(src, dst, ssem, rsem, peer):
        copy = pltpu.make_async_remote_copy(
            src_ref=src, dst_ref=dst, send_sem=ssem, recv_sem=rsem,
            device_id=peer, device_id_type=pl.DeviceIdType.MESH,
        )
        copy.start()
        return copy

    masks_one = tap_masks(32)
    own = jnp.concatenate([vol[p].astype(F32) for p in range(4)], axis=0)
    for v in range(9):
        x1[v * 16:(v + 1) * 16, :] = shifted(own, v, masks_one, 32).astype(BF16)
    x1[224:256, :] = jnp.zeros((32, 1024), BF16)

    pl.semaphore_wait(barrier, len(peers))
    sends = []
    h1_hi = send(vol.at[0], h1.at[0], halo_send.at[0], halo_recv.at[0], (prv, dp))
    h1_lo = send(vol.at[3], h1.at[1], halo_send.at[1], halo_recv.at[1], (nxt, dp))

    k = iota((1, 256), 1)
    is_own = k < 144
    kh = k - 144
    v_k = jnp.where(is_own, k // 16, kh // 8)
    p_k = jnp.where(is_own, (k % 16) // 4 + 1, jnp.where((kh % 8) < 4, 5, 0))
    c_k = k % 4
    row = iota((128, 256), 0)
    for d in range(4):
        kd = p_k - d
        ok = jnp.logical_and(jnp.logical_and(kd >= 0, kd <= 2), k < 216)
        target = jnp.where(ok, c_k * 27 + kd * 9 + v_k, -1)
        tsel[:, d * 256:(d + 1) * 256] = jnp.where(row == target, 1.0, 0.0).astype(BF16)
    for d in range(4):
        w1big[d * 32:(d + 1) * 32, :] = dot(w1[...], tsel[:, d * 256:(d + 1) * 256]).astype(BF16)

    for blk in range(4):
        r = iota((256, 256), 0) + blk * 256
        c = iota((256, 256), 1)
        pool[blk * 256:(blk + 1) * 256, :] = jnp.where(
            c == (r // 64) * 16 + (r % 32) // 2, 1.0, 0.0
        ).astype(BF16)

    zero = jnp.zeros((32, 64), F32)
    for v in range(9):
        w = [w2[kd * 9 + v].astype(F32) for kd in range(3)]
        left = jnp.concatenate([w[0], w[1], w[2], zero], axis=0)
        right = jnp.concatenate([zero, w[0], w[1], w[2]], axis=0)
        both = jnp.concatenate([left, right], axis=1)
        w2band[:, v * 128:(v + 1) * 128] = both.T.astype(BF16)
        top = jnp.concatenate([w[2], w[1], w[0], zero], axis=1)
        bottom = jnp.concatenate([zero, w[2], w[1], w[0]], axis=1)
        wp[v * 64:v * 64 + 32, :] = top.astype(BF16)
        wp[v * 64 + 32:v * 64 + 64, :] = bottom.astype(BF16)
    for d in range(2):
        cotf[d * 64:(d + 1) * 64, :] = cot[d].astype(F32)

    h1_hi.wait()
    h1_lo.wait()
    first = space == 0
    last = space == slabs - 1
    hi = jnp.where(last, 0.0, h1[0].astype(F32))
    lo = jnp.where(first, 0.0, h1[1].astype(F32))
    halo = jnp.concatenate([hi, lo], axis=0)
    parts = [shifted(halo, v, masks_one, 32) for v in range(9)] + [jnp.zeros((8, 1024), F32)]
    for j in range(5):
        x1[144 + 16 * j:160 + 16 * j, :] = jnp.concatenate(
            [parts[2 * j], parts[2 * j + 1]], axis=0
        ).astype(BF16)

    act_hi = []
    act_lo = []
    for dd in range(2):
        total = None
        for d in (2 * dd, 2 * dd + 1):
            pre = dot(w1big[d * 32:(d + 1) * 32, :], x1[...])
            s = sigmoid(pre)
            act = pre * s
            dsilu_one[d * 32:(d + 1) * 32, :] = s * (1.0 + pre * (1.0 - s))
            total = act if total is None else total + act
        high = total.astype(BF16)
        act_hi.append(high)
        act_lo.append((total - high.astype(F32)).astype(BF16))
    sums = dot(jnp.concatenate(act_hi + act_lo, axis=0), pool[...])
    pooled = ((sums[0:64] + sums[64:128]) * 0.125).astype(BF16)
    pext[32:96, :] = pooled
    h2_hi = send(pext.at[32:64], pext.at[96:128], halo_send.at[2], halo_recv.at[2], (prv, dp))
    h2_lo = send(pext.at[64:96], pext.at[0:32], halo_send.at[3], halo_recv.at[3], (nxt, dp))

    masks = tap_masks(16)
    pooled_f = pooled.astype(F32)
    for v in range(9):
        xcol[v * 128 + 32:v * 128 + 96, :] = shifted(pooled_f, v, masks, 16).astype(BF16)
    h2_hi.wait()
    h2_lo.wait()
    hi = jnp.where(last, 0.0, pext[96:128, :].astype(F32))
    lo = jnp.where(first, 0.0, pext[0:32, :].astype(F32))
    for v in range(9):
        xcol[v * 128 + 96:v * 128 + 128, :] = shifted(hi, v, masks, 16).astype(BF16)
        xcol[v * 128:v * 128 + 32, :] = shifted(lo, v, masks, 16).astype(BF16)

    pre = dot(w2band[...], xcol[...])
    s = sigmoid(pre)
    delta = (cotf[...] * (s * (1.0 + pre * (1.0 - s)))).astype(BF16)
    dext[64:192, :] = delta
    h3_hi = send(dext.at[64:128], dext.at[192:256], halo_send.at[4], halo_recv.at[4], (prv, dp))
    h3_lo = send(dext.at[128:192], dext.at[0:64], halo_send.at[5], halo_recv.at[5], (nxt, dp))
    feat[...] = (pre * s).astype(BF16)

    rows_x, rows_y, rows_z = 64 // nx, 64 // (nx * ny), 64 // slabs
    scale_two = 1.0 / 512.0 * math.sqrt(64 * 8 / (slabs * dp_n))
    for v in range(9):
        g = dot_nt(delta, xcol[v * 128:(v + 1) * 128, :])
        g = (g[0:64] + pltpu.roll(g[64:128], 96, 1)) * scale_two
        for i in range(nx):
            piece = g[i * rows_x:(i + 1) * rows_x]
            g2f[i, :, v * 128:(v + 1) * 128] = piece
            g2s[i, :, v * 128:(v + 1) * 128] = piece.astype(BF16)
    g2_x = []
    for r in range(1, nx):
        other, peer = x_peer(r)
        g2_x.append(send(g2s.at[other], g2x.at[r - 1], xs.at[0, r - 1], xr.at[0, r - 1], peer))

    h3_hi.wait()
    h3_lo.wait()
    hi = jnp.where(last, 0.0, dext[192:256, :].astype(F32)).astype(BF16)
    lo = jnp.where(first, 0.0, dext[0:64, :].astype(F32)).astype(BF16)
    z = dot(wp[...], jnp.concatenate([lo, delta, hi], axis=0))
    total = None
    for v in range(9):
        term = shifted(z[v * 64:(v + 1) * 64], v, masks, 16, sign=-1)
        total = term if total is None else total + term
    pg = total.astype(BF16)
    pgrad[...] = pg

    spread = dot_nt(pg, pool[...]) * 0.125
    g1 = None
    for d in range(4):
        dd = d // 2
        one = (spread[dd * 32:(dd + 1) * 32] * dsilu_one[d * 32:(d + 1) * 32, :]).astype(BF16)
        g = dot_nt(one, x1[...])
        hi = g.astype(BF16)
        rest = g - hi.astype(F32)
        mid = rest.astype(BF16)
        low = (rest - mid.astype(F32)).astype(BF16)
        out = dot_nt(jnp.concatenate([hi, mid, low], axis=0), tsel[:, d * 256:(d + 1) * 256])
        out = out[0:32] + (out[32:64] + out[64:96])
        g1 = out if g1 is None else g1 + out
    g1 = g1 * (1.0 / math.sqrt(4096 * slabs * dp_n))
    q_x, q_y = 32 // nx, 32 // (nx * ny)
    for i in range(nx):
        g1s[i] = g1[i * q_x:(i + 1) * q_x]
    g1_x = []
    for r in range(1, nx):
        other, peer = x_peer(r)
        g1_x.append(send(g1s.at[other], g1x.at[r - 1], xs.at[1, r - 1], xr.at[1, r - 1], peer))

    for copy in g2_x:
        copy.wait()
    total = g2f[xi]
    for r in range(nx - 1):
        total = total + g2x[r].astype(F32)
    for i in range(ny):
        piece = total[i * rows_y:(i + 1) * rows_y]
        g2yf[i] = piece
        g2ys[i] = piece.astype(BF16)
    g2_y = []
    for r in range(1, ny):
        other, peer = y_peer(r)
        g2_y.append(send(g2ys.at[other], g2y.at[r - 1], ys.at[0, r - 1], yr.at[0, r - 1], peer))

    for copy in g1_x:
        copy.wait()
    total = g1s[xi]
    for r in range(nx - 1):
        total = total + g1x[r]
    for i in range(ny):
        g1ys[i] = total[i * q_y:(i + 1) * q_y]
    g1_y = []
    for r in range(1, ny):
        other, peer = y_peer(r)
        g1_y.append(send(g1ys.at[other], g1y.at[r - 1], ys.at[1, r - 1], yr.at[1, r - 1], peer))

    for copy in g2_y:
        copy.wait()
    total = g2yf[yi]
    for r in range(ny - 1):
        total = total + g2y[r].astype(F32)
    for i in range(nz):
        g2z[i] = total[i * rows_z:(i + 1) * rows_z]
    g2r[me_z] = g2z[zl]
    g2_z = []
    for r in range(1, team):
        other, oz, peer = z_peer(r)
        g2_z.append(send(g2z.at[oz], g2r.at[me_z], zs.at[0, r - 1], zr.at[0, me_z], peer))

    for copy in g1_y:
        copy.wait()
    total = g1ys[yi]
    for r in range(ny - 1):
        total = total + g1y[r]
    g1z[...] = total
    g1r[me_z] = total
    g1_z = []
    for r in range(1, team):
        other, oz, peer = z_peer(r)
        g1_z.append(send(g1z, g1r.at[me_z], zs.at[1, r - 1], zr.at[1, me_z], peer))

    for r in range(1, team):
        other, oz, peer = z_peer(r)
        g2_z[r - 1].wait_send()
        pltpu.make_async_remote_copy(
            src_ref=g2z.at[zl], dst_ref=g2r.at[other], send_sem=zs.at[0, r - 1],
            recv_sem=zr.at[0, other], device_id=peer, device_id_type=pl.DeviceIdType.MESH,
        ).wait_recv()
    total = g2r[0]
    for r in range(1, team):
        total = total + g2r[r]
    g2_out[...] = total
    for r in range(1, team):
        other, oz, peer = z_peer(r)
        g1_z[r - 1].wait_send()
        pltpu.make_async_remote_copy(
            src_ref=g1z, dst_ref=g1r.at[other], send_sem=zs.at[1, r - 1],
            recv_sem=zr.at[1, other], device_id=peer, device_id_type=pl.DeviceIdType.MESH,
        ).wait_recv()
    total = g1r[0]
    for r in range(1, team):
        total = total + g1r[r]
    g1_out[...] = total


def on_device(sizes, volumes, kernel_one, kernel_two, cotangent):
    nx, ny, nz, dp_n = sizes
    slabs, team = nx * ny * nz, nz * dp_n
    vol = jnp.transpose(volumes[0], (1, 0, 2, 3)).reshape(4, 4, 1024)
    w1 = jnp.pad(kernel_one.reshape(32, 108), ((0, 0), (0, 20)))
    w2 = jnp.transpose(kernel_two, (2, 3, 4, 1, 0)).reshape(27, 32, 64)
    cot = jnp.transpose(cotangent[0], (1, 0, 2))
    rows_x, rows_y, rows_z = 64 // nx, 64 // (nx * ny), 64 // slabs
    q_x, q_y = 32 // nx, 32 // (nx * ny)
    cols = 1152
    vmem = pl.BlockSpec(memory_space=pltpu.VMEM)
    scratch = [
        ((2, 4, 1024), BF16),
        ((256, 1024), BF16),
        ((128, 1024), BF16),
        ((128, 256), BF16),
        ((1024, 256), BF16),
        ((128, 1024), F32),
        ((128, cols), BF16),
        ((576, 256), BF16),
        ((128, 256), F32),
        ((128, 256), BF16),
        ((cols, 256), BF16),
        ((256, 256), BF16),
        ((nx, rows_x, cols), F32),
        ((nx, rows_x, cols), BF16),
        ((nx - 1, rows_x, cols), BF16),
        ((ny, rows_y, cols), F32),
        ((ny, rows_y, cols), BF16),
        ((ny - 1, rows_y, cols), BF16),
        ((nz, rows_z, cols), F32),
        ((team, rows_z, cols), F32),
        ((nx, q_x, 128), F32),
        ((nx - 1, q_x, 128), F32),
        ((ny, q_y, 128), F32),
        ((ny - 1, q_y, 128), F32),
        ((q_y, 128), F32),
        ((team, q_y, 128), F32),
    ]
    dma = pltpu.SemaphoreType.DMA
    feat, pgrad, g1, g2 = pl.pallas_call(
        functools.partial(kernel, sizes),
        out_shape=(
            jax.ShapeDtypeStruct((128, 256), BF16),
            jax.ShapeDtypeStruct((64, 256), BF16),
            jax.ShapeDtypeStruct((q_y, 128), F32),
            jax.ShapeDtypeStruct((rows_z, cols), F32),
        ),
        in_specs=[vmem] * 4,
        out_specs=(vmem,) * 4,
        scratch_shapes=[pltpu.VMEM(shape, dtype) for shape, dtype in scratch] + [
            dma((6,)), dma((6,)),
            dma((2, nx - 1)), dma((2, nx - 1)),
            dma((2, ny - 1)), dma((2, ny - 1)),
            dma((2, team - 1)), dma((2, team)),
        ],
        compiler_params=pltpu.CompilerParams(collective_id=0, has_side_effects=True),
        name="conv_step",
    )(vol, w1, w2, cot)
    features = jnp.transpose(feat.reshape(2, 64, 256), (1, 0, 2))[None]
    pooled_grad = jnp.transpose(pgrad.reshape(2, 32, 256), (1, 0, 2))[None]
    zl = lax.rem(lax.axis_index("space"), nz)
    flat_one = g1[:, :108].reshape(-1)
    half = flat_one.shape[0] // nz
    grad_one = lax.dynamic_slice_in_dim(flat_one, zl * half, half, 0)
    grad_two = jnp.transpose(g2.reshape(rows_z, 9, 4, 32)[:, :, :3], (0, 3, 2, 1)).reshape(-1)
    return features, pooled_grad, grad_one, grad_two


def solution(mesh):
    slabs, dp_n = mesh.shape["space"], mesh.shape["dp"]
    sizes = (4, 8, 2, dp_n) if slabs == 64 else (2, 2, slabs // 4, dp_n)
    in_specs = (P("dp", None, "space", None, None), P(), P(), P("dp", None, "space", None))
    out_specs = (P("dp", None, "space", None), P("dp", None, "space", None), P("space"), P("space"))
    return jax.shard_map(
        functools.partial(on_device, sizes), mesh=mesh, in_specs=in_specs, out_specs=out_specs,
        check_vma=False,
    )
```

```python
import functools
import math

import jax
import jax.numpy as jnp
from jax import lax
from jax.experimental import pallas as pl
from jax.experimental.pallas import tpu as pltpu
from jax.sharding import PartitionSpec as P

F32 = jnp.float32
BF16 = jnp.bfloat16
TAPS = [(a, b) for a in (-1, 0, 1) for b in (-1, 0, 1)]
NT = (((1,), (1,)), ((), ()))


def dot(a, b):
    return jnp.dot(a, b, preferred_element_type=F32)


def dot_nt(a, b):
    return lax.dot_general(a, b, NT, preferred_element_type=F32)


def iota(shape, dim):
    return lax.broadcasted_iota(jnp.int32, shape, dim)


def tap_masks(width):
    lane = iota((1, width * width), 1)
    row, col = lane // width, lane % width
    rows = {-1: row >= 1, 0: None, 1: row < width - 1}
    cols = {-1: col >= 1, 0: None, 1: col < width - 1}
    masks = []
    for dr, dc in TAPS:
        parts = [m for m in (rows[dr], cols[dc]) if m is not None]
        mask = None
        for part in parts:
            mask = part if mask is None else jnp.logical_and(mask, part)
        masks.append(mask)
    return masks


def shifted(block, tap, masks, width, sign=1):
    dr, dc = TAPS[tap]
    dr, dc = sign * dr, sign * dc
    if dr == 0 and dc == 0:
        return block
    size = width * width
    moved = pltpu.roll(block, (-(dr * width + dc)) % size, 1)
    return jnp.where(masks[TAPS.index((dr, dc))], moved, 0.0)


def one_hot(shape, column_of_row):
    return jnp.where(iota(shape, 1) == column_of_row(iota(shape, 0)), 1.0, 0.0).astype(BF16)


def sigmoid(v):
    return 1.0 / (1.0 + jnp.exp(-v))


def kernel(
    sizes,
    vol_in, w1_in, w2_in, cot_in,
    feat_out, pgrad_out, g1_out, g2_out,
    vol, w1, w2, cot, feat, pgrad,
    vrows, vgrp, vnear, vedge, vfar, cots, cotr, w1rows,
    x1, tsel, w1big, pool, dsilu_one, w2band, wp,
    xcol_a, xcol_b,
    g2f, g2s, g2x, g2yf, g2ys, g2y, g2z, g2r,
    g1s, g1x, g1ys, g1y, g1z, g1r,
    local, halo_send, halo_recv, xs, xr, ys, yr, zs, zr,
):
    nx, ny, nz, dp_n = sizes
    slabs = nx * ny * nz
    space = lax.axis_index("space")
    dp = lax.axis_index("dp")
    zl = lax.rem(space, nz)
    xy = lax.div(space, nz)
    yi = lax.rem(xy, ny)
    xi = lax.div(xy, ny)
    nxt = lax.rem(space + 1, slabs)
    prv = lax.rem(space + slabs - 1, slabs)
    nxt2 = lax.rem(space + 2, slabs)
    prv2 = lax.rem(space + slabs - 2, slabs)
    team = nz * dp_n
    me_z = zl * dp_n + dp

    def x_peer(r):
        other = lax.rem(xi + r, nx)
        return other, ((other * ny + yi) * nz + zl, dp)

    def y_peer(r):
        other = lax.rem(yi + r, ny)
        return other, ((xi * ny + other) * nz + zl, dp)

    def z_peer(r):
        other = lax.rem(me_z + r, team)
        oz = lax.div(other, dp_n)
        return other, oz, (xy * nz + oz, lax.rem(other, dp_n))

    barrier = pltpu.get_barrier_semaphore()
    peers = [(nxt, dp), (prv, dp), (nxt2, dp), (prv2, dp)]
    peers += [x_peer(r)[1] for r in range(1, nx)]
    peers += [y_peer(r)[1] for r in range(1, ny)]
    peers += [z_peer(r)[2] for r in range(1, team)]
    for peer in peers:
        pl.semaphore_signal(barrier, inc=1, device_id=peer, device_id_type=pl.DeviceIdType.MESH)

    loads = [
        pltpu.make_async_copy(src, dst, local.at[i])
        for i, (src, dst) in enumerate([(vol_in, vol), (cot_in, cot), (w1_in, w1), (w2_in, w2)])
    ]
    for copy in loads:
        copy.start()

    def send(src, dst, ssem, rsem, peer):
        copy = pltpu.make_async_remote_copy(
            src_ref=src, dst_ref=dst, send_sem=ssem, recv_sem=rsem,
            device_id=peer, device_id_type=pl.DeviceIdType.MESH,
        )
        copy.start()
        return copy

    loads[0].wait()
    for p in range(4):
        for c in range(4):
            vrows[(p * 4 + c) * 32:(p * 4 + c) * 32 + 32, :] = vol[c, p].astype(F32)
    own = jnp.concatenate(
        [
            jnp.concatenate([vrows[pl.ds(4 * j + k, 16, stride=32), :] for k in range(4)], axis=1)
            for j in range(8)
        ],
        axis=1,
    )
    vgrp[...] = own.astype(BF16)
    vedge[0] = own[0:4].astype(BF16)
    vedge[1] = own[12:16].astype(BF16)
    loads[1].wait()
    split = one_hot((128, 128), lambda r: (r % 64) * 2 + r // 64)
    merge = one_hot((128, 128), lambda r: (r % 2) * 64 + r // 2)
    merge_half = one_hot((64, 64), lambda r: (r % 2) * 32 + r // 2)
    own_cot = dot(split, cot[...].reshape(128, 256))
    cots[0] = own_cot[0:64].astype(BF16)
    cots[1] = own_cot[64:128].astype(BF16)

    pl.semaphore_wait(barrier, len(peers))
    halos = [
        send(vgrp, vnear.at[0], halo_send.at[0], halo_recv.at[0], (nxt, dp)),
        send(vgrp, vnear.at[1], halo_send.at[1], halo_recv.at[1], (prv, dp)),
        send(vedge.at[1], vfar.at[0], halo_send.at[2], halo_recv.at[2], (nxt2, dp)),
        send(vedge.at[0], vfar.at[1], halo_send.at[3], halo_recv.at[3], (prv2, dp)),
        send(cots.at[1], cotr.at[0], halo_send.at[4], halo_recv.at[4], (nxt, dp)),
        send(cots.at[0], cotr.at[1], halo_send.at[5], halo_recv.at[5], (prv, dp)),
    ]

    masks_one = tap_masks(32)
    for v in range(9):
        x1[1, v * 16:(v + 1) * 16, :] = shifted(own, v, masks_one, 32).astype(BF16)
    for g in range(3):
        x1[g, 224:256, :] = jnp.zeros((32, 1024), BF16)

    k = iota((1, 256), 1)
    is_own = k < 144
    kh = k - 144
    v_k = jnp.where(is_own, k // 16, kh // 8)
    p_k = jnp.where(is_own, (k % 16) // 4 + 1, jnp.where((kh % 8) < 4, 5, 0))
    c_k = k % 4
    row = iota((128, 256), 0)
    for d in range(4):
        kd = p_k - d
        ok = jnp.logical_and(jnp.logical_and(kd >= 0, kd <= 2), k < 216)
        target = jnp.where(ok, c_k * 27 + kd * 9 + v_k, -1)
        tsel[:, d * 256:(d + 1) * 256] = jnp.where(row == target, 1.0, 0.0).astype(BF16)
    w1rows[...] = jnp.zeros((128, 128), F32)
    loads[2].wait()
    for t in range(27):
        w1rows[pl.ds(t, 4, stride=27), 0:32] = w1[t].astype(F32)
    w1t = w1rows[...].T[0:32].astype(BF16)
    bands = dot(w1t, tsel[...]).astype(BF16)
    for d in range(4):
        w1big[d * 32:(d + 1) * 32, :] = bands[:, d * 256:(d + 1) * 256]

    for blk in range(4):
        r = iota((256, 256), 0) + blk * 256
        pool[blk * 256:(blk + 1) * 256, :] = jnp.where(
            iota((256, 256), 1) == (r // 64) * 16 + (r % 32) // 2, 1.0, 0.0
        ).astype(BF16)

    loads[3].wait()
    zero = jnp.zeros((32, 64), F32)
    for v in range(9):
        w = [w2[kd * 9 + v].astype(F32) for kd in range(3)]
        left = jnp.concatenate([w[0], w[1], w[2], zero], axis=0)
        right = jnp.concatenate([zero, w[0], w[1], w[2]], axis=0)
        both = jnp.concatenate([left, right], axis=1)
        w2band[:, v * 128:(v + 1) * 128] = both.T.astype(BF16)
        top = jnp.concatenate([w[2], w[1], w[0], zero], axis=1)
        bottom = jnp.concatenate([zero, w[2], w[1], w[0]], axis=1)
        wp[v * 64:v * 64 + 32, :] = top.astype(BF16)
        wp[v * 64 + 32:v * 64 + 64, :] = bottom.astype(BF16)

    for copy in halos[0:4]:
        copy.wait()
    first, last = space == 0, space == slabs - 1
    groups = [
        jnp.where(first, 0.0, vnear[0].astype(F32)),
        own,
        jnp.where(last, 0.0, vnear[1].astype(F32)),
    ]
    far_lo = jnp.where(space <= 1, 0.0, vfar[0].astype(F32))
    far_hi = jnp.where(space >= slabs - 2, 0.0, vfar[1].astype(F32))
    below = [far_lo, groups[0][12:16], own[12:16]]
    above = [own[0:4], groups[2][0:4], far_hi]
    masks = tap_masks(16)
    for g in (0, 2, 1):
        if g != 1:
            for v in range(9):
                x1[g, v * 16:(v + 1) * 16, :] = shifted(groups[g], v, masks_one, 32).astype(BF16)
        halo = jnp.concatenate([above[g], below[g]], axis=0)
        parts = [shifted(halo, v, masks_one, 32) for v in range(9)] + [jnp.zeros((8, 1024), F32)]
        for j in range(5):
            x1[g, 144 + 16 * j:160 + 16 * j, :] = jnp.concatenate(
                [parts[2 * j], parts[2 * j + 1]], axis=0
            ).astype(BF16)
        sums = None
        for n in range(4):
            lanes = slice(n * 256, (n + 1) * 256)
            pre = dot(w1big[...], x1[g, :, lanes])
            s = sigmoid(pre)
            act = pre * s
            if g == 1:
                dsilu_one[:, lanes] = s * (1.0 + pre * (1.0 - s))
            total = jnp.concatenate([act[0:32] + act[32:64], act[64:96] + act[96:128]], axis=0)
            high = total.astype(BF16)
            low = (total - high.astype(F32)).astype(BF16)
            part = dot(jnp.concatenate([high, low], axis=0), pool[lanes, :])
            sums = part if sums is None else sums + part
        pooled = ((sums[0:64] + sums[64:128]) * 0.125).astype(BF16).astype(F32)
        if g == 0:
            pooled = jnp.where(first, 0.0, pooled)
        if g == 2:
            pooled = jnp.where(last, 0.0, pooled)
        for v in range(9):
            block = shifted(pooled, v, masks, 16).astype(BF16)
            if g < 2:
                xcol_a[v * 128 + g * 64:v * 128 + g * 64 + 64, :] = block
            if g > 0:
                xcol_b[v * 128 + g * 64 - 64:v * 128 + g * 64, :] = block

    halos[4].wait()
    halos[5].wait()
    cot_a = jnp.concatenate([cotr[0].astype(F32), cots[0].astype(F32)], axis=0)
    cot_b = jnp.concatenate([cots[1].astype(F32), cotr[1].astype(F32)], axis=0)
    pre_a = dot(w2band[...], xcol_a[...])
    s_a = sigmoid(pre_a)
    delta_a = cot_a * (s_a * (1.0 + pre_a * (1.0 - s_a)))
    pre_b = dot(w2band[...], xcol_b[...])
    s_b = sigmoid(pre_b)
    delta_b = cot_b * (s_b * (1.0 + pre_b * (1.0 - s_b)))
    delta = jnp.concatenate(
        [
            jnp.where(first, 0.0, delta_a[0:64]),
            delta_a[64:128],
            delta_b[0:64],
            jnp.where(last, 0.0, delta_b[64:128]),
        ],
        axis=0,
    ).astype(BF16)

    rows_x, rows_y, rows_z = 64 // nx, 64 // (nx * ny), 64 // slabs
    scale_two = 1.0 / 512.0 * math.sqrt(64 * 8 / (slabs * dp_n))
    for v in range(9):
        lower = dot_nt(delta[64:128], xcol_a[v * 128:(v + 1) * 128, :])
        upper = dot_nt(delta[128:192], xcol_b[v * 128:(v + 1) * 128, :])
        g = (pltpu.roll(lower, 96, 1) + upper) * scale_two
        for i in range(nx):
            piece = g[i * rows_x:(i + 1) * rows_x]
            g2f[i, :, v * 128:(v + 1) * 128] = piece
            g2s[i, :, v * 128:(v + 1) * 128] = piece.astype(BF16)
    g2_x = []
    for r in range(1, nx):
        other, peer = x_peer(r)
        g2_x.append(send(g2s.at[other], g2x.at[r - 1], xs.at[0, r - 1], xr.at[0, r - 1], peer))

    z = dot(wp[...], delta)
    total = None
    for v in range(9):
        term = shifted(z[v * 64:(v + 1) * 64], v, masks, 16, sign=-1)
        total = term if total is None else total + term
    pg = total.astype(BF16)

    g1k = None
    for n in range(4):
        lanes = slice(n * 256, (n + 1) * 256)
        spread = dot_nt(pg, pool[lanes, :]) * 0.125
        twice = jnp.concatenate([spread[0:32], spread[0:32], spread[32:64], spread[32:64]], axis=0)
        one = (twice * dsilu_one[:, lanes]).astype(BF16)
        part = dot_nt(one, x1[1, :, lanes])
        g1k = part if g1k is None else g1k + part
    hi = g1k.astype(BF16)
    mid = (g1k - hi.astype(F32)).astype(BF16)
    g1 = None
    for d in range(4):
        rows = slice(d * 32, (d + 1) * 32)
        out = dot_nt(jnp.concatenate([hi[rows], mid[rows]], axis=0), tsel[:, d * 256:(d + 1) * 256])
        g1 = out if g1 is None else g1 + out
    g1 = (g1[0:32] + g1[32:64]) * (1.0 / math.sqrt(4096 * slabs * dp_n))
    q_x, q_y = 32 // nx, 32 // (nx * ny)
    for i in range(nx):
        g1s[i] = g1[i * q_x:(i + 1) * q_x]
    g1_x = []
    for r in range(1, nx):
        other, peer = x_peer(r)
        g1_x.append(send(g1s.at[other], g1x.at[r - 1], xs.at[1, r - 1], xr.at[1, r - 1], peer))

    own_feat = jnp.concatenate([(pre_a * s_a)[64:128], (pre_b * s_b)[0:64]], axis=0).astype(BF16)
    feat[...] = dot(merge, own_feat).astype(BF16).reshape(64, 2, 256)
    pgrad[...] = dot(merge_half, pg).astype(BF16).reshape(32, 2, 256)
    stores = [
        pltpu.make_async_copy(feat, feat_out, local.at[4]),
        pltpu.make_async_copy(pgrad, pgrad_out, local.at[5]),
    ]
    for copy in stores:
        copy.start()

    for copy in g2_x:
        copy.wait()
    total = g2f[xi]
    for r in range(nx - 1):
        total = total + g2x[r].astype(F32)
    for i in range(ny):
        piece = total[i * rows_y:(i + 1) * rows_y]
        g2yf[i] = piece
        g2ys[i] = piece.astype(BF16)
    g2_y = []
    for r in range(1, ny):
        other, peer = y_peer(r)
        g2_y.append(send(g2ys.at[other], g2y.at[r - 1], ys.at[0, r - 1], yr.at[0, r - 1], peer))

    for copy in g1_x:
        copy.wait()
    total = g1s[xi]
    for r in range(nx - 1):
        total = total + g1x[r]
    for i in range(ny):
        g1ys[i] = total[i * q_y:(i + 1) * q_y]
    g1_y = []
    for r in range(1, ny):
        other, peer = y_peer(r)
        g1_y.append(send(g1ys.at[other], g1y.at[r - 1], ys.at[1, r - 1], yr.at[1, r - 1], peer))

    for copy in g2_y:
        copy.wait()
    total = g2yf[yi]
    for r in range(ny - 1):
        total = total + g2y[r].astype(F32)
    for i in range(nz):
        g2z[i] = total[i * rows_z:(i + 1) * rows_z]
    g2r[me_z] = g2z[zl]
    g2_z = []
    for r in range(1, team):
        other, oz, peer = z_peer(r)
        g2_z.append(send(g2z.at[oz], g2r.at[me_z], zs.at[0, r - 1], zr.at[0, me_z], peer))

    for copy in g1_y:
        copy.wait()
    total = g1ys[yi]
    for r in range(ny - 1):
        total = total + g1y[r]
    g1z[...] = total
    g1r[me_z] = total
    g1_z = []
    for r in range(1, team):
        other, oz, peer = z_peer(r)
        g1_z.append(send(g1z, g1r.at[me_z], zs.at[1, r - 1], zr.at[1, me_z], peer))

    for r in range(1, team):
        other, oz, peer = z_peer(r)
        g2_z[r - 1].wait_send()
        pltpu.make_async_remote_copy(
            src_ref=g2z.at[zl], dst_ref=g2r.at[other], send_sem=zs.at[0, r - 1],
            recv_sem=zr.at[0, other], device_id=peer, device_id_type=pl.DeviceIdType.MESH,
        ).wait_recv()
    total = g2r[0]
    for r in range(1, team):
        total = total + g2r[r]
    g2_out[...] = total
    for r in range(1, team):
        other, oz, peer = z_peer(r)
        g1_z[r - 1].wait_send()
        pltpu.make_async_remote_copy(
            src_ref=g1z, dst_ref=g1r.at[other], send_sem=zs.at[1, r - 1],
            recv_sem=zr.at[1, other], device_id=peer, device_id_type=pl.DeviceIdType.MESH,
        ).wait_recv()
    total = g1r[0]
    for r in range(1, team):
        total = total + g1r[r]
    g1_out[...] = total
    for copy in stores:
        copy.wait()


def on_device(sizes, volumes, kernel_one, kernel_two, cotangent):
    nx, ny, nz, dp_n = sizes
    slabs, team = nx * ny * nz, nz * dp_n
    w1 = jnp.transpose(kernel_one, (2, 3, 4, 1, 0)).reshape(27, 4, 32)
    w2 = jnp.transpose(kernel_two, (2, 3, 4, 1, 0)).reshape(27, 32, 64)
    rows_x, rows_y, rows_z = 64 // nx, 64 // (nx * ny), 64 // slabs
    q_x, q_y = 32 // nx, 32 // (nx * ny)
    cols = 1152
    vmem = pl.BlockSpec(memory_space=pltpu.VMEM)
    hbm = pl.BlockSpec(memory_space=pl.ANY)
    scratch = [
        ((4, 4, 32, 32), BF16),
        ((27, 4, 32), BF16),
        ((27, 32, 64), BF16),
        ((64, 2, 256), BF16),
        ((64, 2, 256), BF16),
        ((32, 2, 256), BF16),
        ((512, 32), F32),
        ((16, 1024), BF16),
        ((2, 16, 1024), BF16),
        ((2, 4, 1024), BF16),
        ((2, 4, 1024), BF16),
        ((2, 64, 256), BF16),
        ((2, 64, 256), BF16),
        ((128, 128), F32),
        ((3, 256, 1024), BF16),
        ((128, 1024), BF16),
        ((128, 256), BF16),
        ((1024, 256), BF16),
        ((128, 1024), F32),
        ((128, cols), BF16),
        ((576, 256), BF16),
        ((cols, 256), BF16),
        ((cols, 256), BF16),
        ((nx, rows_x, cols), F32),
        ((nx, rows_x, cols), BF16),
        ((nx - 1, rows_x, cols), BF16),
        ((ny, rows_y, cols), F32),
        ((ny, rows_y, cols), BF16),
        ((ny - 1, rows_y, cols), BF16),
        ((nz, rows_z, cols), F32),
        ((team, rows_z, cols), F32),
        ((nx, q_x, 128), F32),
        ((nx - 1, q_x, 128), F32),
        ((ny, q_y, 128), F32),
        ((ny - 1, q_y, 128), F32),
        ((q_y, 128), F32),
        ((team, q_y, 128), F32),
    ]
    dma = pltpu.SemaphoreType.DMA
    features, pooled_grad, g1, g2 = pl.pallas_call(
        functools.partial(kernel, sizes),
        out_shape=(
            jax.ShapeDtypeStruct((64, 2, 256), BF16),
            jax.ShapeDtypeStruct((32, 2, 256), BF16),
            jax.ShapeDtypeStruct((q_y, 128), F32),
            jax.ShapeDtypeStruct((rows_z, cols), F32),
        ),
        in_specs=[hbm] * 4,
        out_specs=(hbm, hbm, vmem, vmem),
        scratch_shapes=[pltpu.VMEM(shape, dtype) for shape, dtype in scratch] + [
            dma((6,)), dma((6,)), dma((6,)),
            dma((2, nx - 1)), dma((2, nx - 1)),
            dma((2, ny - 1)), dma((2, ny - 1)),
            dma((2, team - 1)), dma((2, team)),
        ],
        compiler_params=pltpu.CompilerParams(collective_id=0, has_side_effects=True),
        name="conv_step",
    )(volumes[0], w1, w2, cotangent[0])
    zl = lax.rem(lax.axis_index("space"), nz)
    flat_one = g1[:, :108].reshape(-1)
    half = flat_one.shape[0] // nz
    grad_one = lax.dynamic_slice_in_dim(flat_one, zl * half, half, 0)
    grad_two = jnp.transpose(g2.reshape(rows_z, 9, 4, 32)[:, :, :3], (0, 3, 2, 1)).reshape(-1)
    return features[None], pooled_grad[None], grad_one, grad_two


def solution(mesh):
    slabs, dp_n = mesh.shape["space"], mesh.shape["dp"]
    sizes = (4, 8, 2, dp_n) if slabs == 64 else (2, 2, slabs // 4, dp_n)
    in_specs = (P("dp", None, "space", None, None), P(), P(), P("dp", None, "space", None))
    out_specs = (P("dp", None, "space", None), P("dp", None, "space", None), P("space"), P("space"))
    return jax.shard_map(
        functools.partial(on_device, sizes), mesh=mesh, in_specs=in_specs, out_specs=out_specs,
        check_vma=False,
    )
```

```python
import functools
import math

import jax
import jax.numpy as jnp
from jax import lax
from jax.experimental import pallas as pl
from jax.experimental.pallas import tpu as pltpu
from jax.sharding import PartitionSpec as P

F32 = jnp.float32
BF16 = jnp.bfloat16
TAPS = [(a, b) for a in (-1, 0, 1) for b in (-1, 0, 1)]
NT = (((1,), (1,)), ((), ()))


def dot(a, b):
    return jnp.dot(a, b, preferred_element_type=F32)


def dot_nt(a, b):
    return lax.dot_general(a, b, NT, preferred_element_type=F32)


def iota(shape, dim):
    return lax.broadcasted_iota(jnp.int32, shape, dim)


def tap_masks(width):
    lane = iota((1, width * width), 1)
    row, col = lane // width, lane % width
    rows = {-1: row >= 1, 0: None, 1: row < width - 1}
    cols = {-1: col >= 1, 0: None, 1: col < width - 1}
    masks = []
    for dr, dc in TAPS:
        parts = [m for m in (rows[dr], cols[dc]) if m is not None]
        mask = None
        for part in parts:
            mask = part if mask is None else jnp.logical_and(mask, part)
        masks.append(mask)
    return masks


def shifted(block, tap, masks, width, sign=1):
    dr, dc = TAPS[tap]
    dr, dc = sign * dr, sign * dc
    if dr == 0 and dc == 0:
        return block
    size = width * width
    moved = pltpu.roll(block, (-(dr * width + dc)) % size, 1)
    return jnp.where(masks[TAPS.index((dr, dc))], moved, jnp.zeros_like(moved))


def one_hot(shape, column_of_row):
    return jnp.where(iota(shape, 1) == column_of_row(iota(shape, 0)), 1.0, 0.0).astype(BF16)


def silu_parts(half):
    t = jnp.tanh(half)
    return half + half * t, 0.5 + 0.5 * t


def kernel(
    sizes, cols,
    vol_in, w1_in, w2_in, cot_in,
    feat, pgrad, g1_out, g2_out,
    vol, w1, w2, cot,
    vrows, planes, cots, cotr, w1rows,
    x1, tsel, w1big, pool, dsilu_one, w2band, wp, place,
    xcol_a, xcol_b,
    g2s, g2x, g2z, g2r,
    g1s, g1x, g1z, g1r,
    local, halo_send, halo_recv, xs, xr, zs, zr,
):
    nx, ny, nz, dp_n = sizes
    slabs = nx * ny * nz
    space = lax.axis_index("space")
    dp = lax.axis_index("dp")
    zl = lax.rem(space, nz)
    xy = lax.div(space, nz)
    tiles_n = nx * ny
    nxt = lax.rem(space + 1, slabs)
    prv = lax.rem(space + slabs - 1, slabs)
    nxt2 = lax.rem(space + 2, slabs)
    prv2 = lax.rem(space + slabs - 2, slabs)
    team = nz * dp_n
    me_z = zl * dp_n + dp

    def xy_peer(r):
        other = lax.rem(xy + r, tiles_n)
        return other, (other * nz + zl, dp)

    def z_peer(r):
        other = lax.rem(me_z + r, team)
        oz = lax.div(other, dp_n)
        return other, oz, (xy * nz + oz, lax.rem(other, dp_n))

    loads = [
        pltpu.make_async_copy(src, dst, local.at[i])
        for i, (src, dst) in enumerate([(vol_in, vol), (cot_in, cot), (w1_in, w1), (w2_in, w2)])
    ]
    for copy in loads:
        copy.start()
    barrier = pltpu.get_barrier_semaphore()
    peers = [(nxt, dp), (prv, dp), (nxt2, dp), (prv2, dp)]
    peers += [xy_peer(r)[1] for r in range(1, tiles_n)]
    peers += [z_peer(r)[2] for r in range(1, team)]
    for peer in peers:
        pl.semaphore_signal(barrier, inc=1, device_id=peer, device_id_type=pl.DeviceIdType.MESH)

    def send(src, dst, ssem, rsem, peer):
        copy = pltpu.make_async_remote_copy(
            src_ref=src, dst_ref=dst, send_sem=ssem, recv_sem=rsem,
            device_id=peer, device_id_type=pl.DeviceIdType.MESH,
        )
        copy.start()
        return copy

    loads[0].wait()
    for p in range(4):
        for c in range(4):
            vrows[(p * 4 + c) * 32:(p * 4 + c) * 32 + 32, :] = vol[c, p].astype(F32)
    own = jnp.concatenate(
        [
            jnp.concatenate([vrows[pl.ds(4 * j + k, 16, stride=32), :] for k in range(4)], axis=1)
            for j in range(8)
        ],
        axis=1,
    )
    planes[5:9] = own.astype(BF16).reshape(4, 4, 1024)
    planes[14:16] = jnp.zeros((2, 4, 1024), BF16)
    loads[1].wait()
    split = one_hot((128, 128), lambda r: (r % 64) * 2 + r // 64)
    merge = one_hot((128, 128), lambda r: (r % 2) * 64 + r // 2)
    merge_half = one_hot((64, 64), lambda r: (r % 2) * 32 + r // 2)
    own_cot = dot(split, cot[...].reshape(128, 256))
    cots[0] = own_cot[0:64].astype(BF16)
    cots[1] = own_cot[64:128].astype(BF16)

    pl.semaphore_wait(barrier, len(peers))
    halos = [
        send(planes.at[5:9], planes.at[1:5], halo_send.at[0], halo_recv.at[0], (nxt, dp)),
        send(planes.at[5:9], planes.at[9:13], halo_send.at[1], halo_recv.at[1], (prv, dp)),
        send(planes.at[8], planes.at[0], halo_send.at[2], halo_recv.at[2], (nxt2, dp)),
        send(planes.at[5], planes.at[13], halo_send.at[3], halo_recv.at[3], (prv2, dp)),
        send(cots.at[1], cotr.at[0], halo_send.at[4], halo_recv.at[4], (nxt, dp)),
        send(cots.at[0], cotr.at[1], halo_send.at[5], halo_recv.at[5], (prv, dp)),
    ]

    k = iota((1, 224), 1)
    m = k % 48
    odd = jnp.logical_and(m >= 24, k < 192)
    v_k = (k // 48) * 2 + jnp.where(odd, 1, 0)
    p_k = jnp.where(odd, jnp.where(m < 32, m // 4 - 2, m // 4 - 8), m // 4)
    for d in range(4):
        kd = p_k - d
        ok = jnp.logical_and(kd >= 0, kd <= 2)
        target = jnp.where(ok, (k % 4) * 27 + kd * 9 + v_k, -1)
        tsel[d] = jnp.where(iota((128, 224), 0) == target, 1.0, 0.0).astype(BF16)
    w1rows[...] = jnp.zeros((128, 128), F32)
    loads[2].wait()
    for t in range(27):
        w1rows[pl.ds(t, 4, stride=27), 0:32] = w1[t].astype(F32)
    w1t = w1rows[...].T[0:32].astype(BF16)
    for d in range(4):
        w1big[d * 32:(d + 1) * 32, :] = (0.5 * dot(w1t, tsel[d])).astype(BF16)

    for blk in range(4):
        r = iota((256, 256), 0) + blk * 256
        pool[blk * 256:(blk + 1) * 256, :] = jnp.where(
            iota((256, 256), 1) == (r // 64) * 16 + (r % 32) // 2, 1.0, 0.0
        ).astype(BF16)

    loads[3].wait()
    zero = jnp.zeros((32, 64), F32)
    for v in range(9):
        w = [w2[kd * 9 + v].astype(F32) for kd in range(3)]
        left = jnp.concatenate([w[0], w[1], w[2], zero], axis=0)
        right = jnp.concatenate([zero, w[0], w[1], w[2]], axis=0)
        both = jnp.concatenate([left, right], axis=1)
        w2band[:, v * 128:(v + 1) * 128] = (0.5 * both.T).astype(BF16)
        top = jnp.concatenate([w[2], w[1], w[0], zero], axis=1)
        bottom = jnp.concatenate([zero, w[2], w[1], w[0]], axis=1)
        wp[v * 64:v * 64 + 32, :] = top.astype(BF16)
        wp[v * 64 + 32:v * 64 + 64, :] = bottom.astype(BF16)

    for copy in halos[0:4]:
        copy.wait_recv()
    first, last = space == 0, space == slabs - 1
    row = iota((64, 1), 0) // 4
    inside = jnp.logical_and(row >= 5 - 4 * space, row < 5 + 4 * (slabs - space))
    field = jnp.where(inside, planes[...].reshape(64, 1024).astype(F32), 0.0).astype(BF16)
    masks_one = tap_masks(32)
    blocks = []
    for v in range(9):
        blocks.append(shifted(field, v, masks_one, 32))
        if v % 2 == 0 and v < 8:
            continue
        for g in range(3):
            top, mid, low = g * 16, g * 16 + 16, g * 16 + 24
            if v == 8:
                x1[g, 192:224, :] = blocks[8][top:top + 32]
                continue
            base = (v // 2) * 48
            x1[g, base:base + 16, :] = blocks[v - 1][top:mid]
            x1[g, base + 16:base + 32, :] = jnp.concatenate(
                [blocks[v - 1][mid:low], blocks[v][mid:low]], axis=0
            )
            x1[g, base + 32:base + 48, :] = blocks[v][top:mid]
    masks = tap_masks(16)
    for g in (0, 2, 1):
        sums = None
        for n in range(4):
            lanes = slice(n * 256, (n + 1) * 256)
            act, s = silu_parts(dot(w1big[...], x1[g, :, lanes]))
            if g == 1:
                dsilu_one[:, lanes] = s + act * (1.0 - s)
            total = jnp.concatenate([act[0:32] + act[32:64], act[64:96] + act[96:128]], axis=0)
            high = total.astype(BF16)
            low = (total - high.astype(F32)).astype(BF16)
            part = dot(jnp.concatenate([high, low], axis=0), pool[lanes, :])
            sums = part if sums is None else sums + part
        pooled = (sums[0:64] + sums[64:128]) * 0.125
        if g == 0:
            pooled = jnp.where(first, 0.0, pooled)
        if g == 2:
            pooled = jnp.where(last, 0.0, pooled)
        pooled = pooled.astype(BF16)
        for v in range(9):
            block = shifted(pooled, v, masks, 16)
            if g < 2:
                xcol_a[v * 128 + g * 64:v * 128 + g * 64 + 64, :] = block
            if g > 0:
                xcol_b[v * 128 + g * 64 - 64:v * 128 + g * 64, :] = block

    halos[4].wait_recv()
    halos[5].wait_recv()
    cot_a = jnp.concatenate([cotr[0].astype(F32), cots[0].astype(F32)], axis=0)
    cot_b = jnp.concatenate([cots[1].astype(F32), cotr[1].astype(F32)], axis=0)
    act_a, s_a = silu_parts(dot(w2band[...], xcol_a[...]))
    delta_a = cot_a * (s_a + act_a * (1.0 - s_a))
    act_b, s_b = silu_parts(dot(w2band[...], xcol_b[...]))
    delta_b = cot_b * (s_b + act_b * (1.0 - s_b))
    delta = jnp.concatenate(
        [
            jnp.where(first, 0.0, delta_a[0:64]),
            delta_a[64:128],
            delta_b[0:64],
            jnp.where(last, 0.0, delta_b[64:128]),
        ],
        axis=0,
    ).astype(BF16)

    rows_xy, rows_z = 64 // tiles_n, 64 // slabs
    scale_two = 1.0 / 512.0 * math.sqrt(64 * 8 / (slabs * dp_n))
    lower = dot_nt(delta[64:128], xcol_a[...])
    upper = dot_nt(delta[128:192], xcol_b[...])
    tiles = []
    for v in range(9):
        lanes = slice(v * 128, (v + 1) * 128)
        tiles.append(pltpu.roll(lower[:, lanes], 96, 1) + upper[:, lanes])
    lane = iota((1, 128), 1)
    for v in range(7):
        tile = tiles[v]
        if v < 6:
            kd = v % 3
            tile = jnp.where(lane < 96, tile, pltpu.roll(tiles[7 + v // 3], 96 - kd * 32, 1))
        g2s[:, :, v * 128:(v + 1) * 128] = (tile * scale_two).astype(BF16).reshape(tiles_n, rows_xy, 128)
    g2_x = []
    for r in range(1, tiles_n):
        other, peer = xy_peer(r)
        g2_x.append(send(g2s.at[other], g2x.at[xy], xs.at[0, r - 1], xr.at[0, xy], peer))
    for copy in halos:
        copy.wait_send()

    z = dot(wp[...], delta)
    total = None
    for v in range(9):
        term = shifted(z[v * 64:(v + 1) * 64], v, masks, 16, sign=-1)
        total = term if total is None else total + term
    pg = total.astype(BF16)

    g1k = None
    for n in range(4):
        lanes = slice(n * 256, (n + 1) * 256)
        spread = dot_nt(pg, pool[lanes, :]) * 0.125
        twice = jnp.concatenate([spread[0:32], spread[0:32], spread[32:64], spread[32:64]], axis=0)
        one = (twice * dsilu_one[:, lanes]).astype(BF16)
        part = dot_nt(one, x1[1, :, lanes])
        g1k = part if g1k is None else g1k + part
    hi = g1k.astype(BF16)
    mid = (g1k - hi.astype(F32)).astype(BF16)
    g1 = None
    for d in range(4):
        rows = slice(d * 32, (d + 1) * 32)
        out = dot_nt(jnp.concatenate([hi[rows], mid[rows]], axis=0), tsel[d])
        g1 = out if g1 is None else g1 + out
    g1 = (g1[0:32] + g1[32:64]) * (1.0 / math.sqrt(4096 * slabs * dp_n))
    q_y = 32 // tiles_n
    g1s[...] = g1.reshape(tiles_n, q_y, 128)
    g1_x = []
    for r in range(1, tiles_n):
        other, peer = xy_peer(r)
        g1_x.append(send(g1s.at[other], g1x.at[xy], xs.at[1, r - 1], xr.at[1, xy], peer))
    g2x[xy] = g2s[xy]
    g1x[xy] = g1s[xy]

    own_feat = jnp.concatenate([act_a[64:128], act_b[0:64]], axis=0).astype(BF16)
    feat[...] = dot(merge, own_feat).astype(BF16).reshape(64, 2, 256)
    pgrad[...] = dot(merge_half, pg).astype(BF16).reshape(32, 2, 256)

    f = iota((1, 896), 1)
    f_v, f_kd, f_c = f % 9, (f % 27) // 9, f // 27
    f_row = jnp.where(f_v < 7, f_v, (f_v - 7) * 3 + f_kd)
    f_lane = jnp.where(f < 864, jnp.where(f_v < 7, f_kd * 32 + f_c, 96 + f_c), -1)
    place[...] = jnp.where(iota((128, 896), 0) == f_lane, 1.0, 0.0).astype(BF16)

    for r in range(1, tiles_n):
        other, peer = xy_peer(r)
        g2_x[r - 1].wait_send()
        pltpu.make_async_remote_copy(
            src_ref=g2s.at[xy], dst_ref=g2x.at[other], send_sem=xs.at[0, r - 1],
            recv_sem=xr.at[0, other], device_id=peer, device_id_type=pl.DeviceIdType.MESH,
        ).wait_recv()
    parts = g2x[...].reshape(64, cols).astype(F32)
    step = 64
    while step > max(rows_xy, 8):
        step //= 2
        parts = parts[0:step] + parts[step:2 * step]
    total = parts[0:rows_xy]
    for i in range(1, step // rows_xy):
        total = total + parts[i * rows_xy:(i + 1) * rows_xy]
    for i in range(nz):
        rows = []
        for q in range(i * rows_z, (i + 1) * rows_z):
            rows += [total[q:q + 1, v * 128:(v + 1) * 128] for v in range(7)] + [jnp.zeros((1, 128), F32)]
        g2z[i] = jnp.concatenate(rows, axis=0).astype(BF16)
    g2r[me_z] = g2z[zl]
    g2_z = []
    for r in range(1, team):
        other, oz, peer = z_peer(r)
        g2_z.append(send(g2z.at[oz], g2r.at[me_z], zs.at[0, r - 1], zr.at[0, me_z], peer))

    for r in range(1, tiles_n):
        other, peer = xy_peer(r)
        g1_x[r - 1].wait_send()
        pltpu.make_async_remote_copy(
            src_ref=g1s.at[xy], dst_ref=g1x.at[other], send_sem=xs.at[1, r - 1],
            recv_sem=xr.at[1, other], device_id=peer, device_id_type=pl.DeviceIdType.MESH,
        ).wait_recv()
    parts = g1x[...].reshape(32, 128)
    step = 32
    while step > max(q_y, 8):
        step //= 2
        parts = parts[0:step] + parts[step:2 * step]
    total = parts[0:q_y]
    for i in range(1, step // q_y):
        total = total + parts[i * q_y:(i + 1) * q_y]
    g1z[...] = total
    g1r[me_z] = total
    g1_z = []
    for r in range(1, team):
        other, oz, peer = z_peer(r)
        g1_z.append(send(g1z, g1r.at[me_z], zs.at[1, r - 1], zr.at[1, me_z], peer))

    for r in range(1, team):
        other, oz, peer = z_peer(r)
        g2_z[r - 1].wait_send()
        pltpu.make_async_remote_copy(
            src_ref=g2z.at[zl], dst_ref=g2r.at[other], send_sem=zs.at[0, r - 1],
            recv_sem=zr.at[0, other], device_id=peer, device_id_type=pl.DeviceIdType.MESH,
        ).wait_recv()
    total = g2r[0].astype(F32)
    for r in range(1, team):
        total = total + g2r[r].astype(F32)
    for q in range(rows_z):
        packed = total[q * 8:q * 8 + 8]
        hi = packed.astype(BF16)
        rest = packed - hi.astype(F32)
        mid = rest.astype(BF16)
        low = (rest - mid.astype(F32)).astype(BF16)
        split3 = jnp.concatenate([hi.astype(F32), mid.astype(F32), low.astype(F32)], axis=0)
        spread = dot(split3.astype(BF16), place[...])
        spread = spread[0:8] + (spread[8:16] + spread[16:24])
        spread = jnp.where(iota((8, 896), 0) == f_row, spread, 0.0)
        g2_out[q:q + 1, :] = jnp.sum(spread, axis=0, keepdims=True)
    for r in range(1, team):
        other, oz, peer = z_peer(r)
        g1_z[r - 1].wait_send()
        pltpu.make_async_remote_copy(
            src_ref=g1z, dst_ref=g1r.at[other], send_sem=zs.at[1, r - 1],
            recv_sem=zr.at[1, other], device_id=peer, device_id_type=pl.DeviceIdType.MESH,
        ).wait_recv()
    total = g1r[0]
    for r in range(1, team):
        total = total + g1r[r]
    if q_y == 1:
        total = jnp.where(zl == 0, total, pltpu.roll(total, 128 - 54, 1))
    g1_out[...] = total


def finish(feat, pgrad, g1, g2, feat_out, pgrad_out, g1_out, g2_out, one, two, sems):
    copies = [
        pltpu.make_async_copy(feat, feat_out, sems.at[0]),
        pltpu.make_async_copy(pgrad, pgrad_out, sems.at[1]),
    ]
    for copy in copies:
        copy.start()
    one[...] = g1[0, 0:54]
    two[...] = g2[0, 0:864]
    tails = [
        pltpu.make_async_copy(one, g1_out, sems.at[2]),
        pltpu.make_async_copy(two, g2_out, sems.at[3]),
    ]
    for copy in tails:
        copy.start()
    for copy in copies + tails:
        copy.wait()


def on_device(sizes, volumes, kernel_one, kernel_two, cotangent):
    nx, ny, nz, dp_n = sizes
    slabs, team = nx * ny * nz, nz * dp_n
    w1 = jnp.transpose(kernel_one, (2, 3, 4, 1, 0)).reshape(27, 4, 32)
    w2 = jnp.transpose(kernel_two, (2, 3, 4, 1, 0)).reshape(27, 32, 64)
    tiles_n = nx * ny
    rows_xy, rows_z, q_y = 64 // tiles_n, 64 // slabs, 32 // tiles_n
    cols = 896
    vmem = pl.BlockSpec(memory_space=pltpu.VMEM)
    hbm = pl.BlockSpec(memory_space=pltpu.HBM)
    scratch = [
        ((4, 4, 32, 32), BF16),
        ((27, 4, 32), BF16),
        ((27, 32, 64), BF16),
        ((64, 2, 256), BF16),
        ((512, 32), F32),
        ((16, 4, 1024), BF16),
        ((2, 64, 256), BF16),
        ((2, 64, 256), BF16),
        ((128, 128), F32),
        ((3, 224, 1024), BF16),
        ((4, 128, 224), BF16),
        ((128, 224), BF16),
        ((1024, 256), BF16),
        ((128, 1024), F32),
        ((128, 1152), BF16),
        ((576, 256), BF16),
        ((128, cols), BF16),
        ((1152, 256), BF16),
        ((1152, 256), BF16),
        ((tiles_n, rows_xy, cols), BF16),
        ((tiles_n, rows_xy, cols), BF16),
        ((nz, rows_z * 8, 128), BF16),
        ((team, rows_z * 8, 128), BF16),
        ((tiles_n, q_y, 128), F32),
        ((tiles_n, q_y, 128), F32),
        ((q_y, 128), F32),
        ((team, q_y, 128), F32),
    ]
    dma = pltpu.SemaphoreType.DMA
    features, pooled_grad, g1, g2 = pl.pallas_call(
        functools.partial(kernel, sizes, cols),
        out_shape=(
            jax.ShapeDtypeStruct((64, 2, 256), BF16),
            jax.ShapeDtypeStruct((32, 2, 256), BF16),
            jax.ShapeDtypeStruct((q_y, 128), F32),
            jax.ShapeDtypeStruct((rows_z, cols), F32),
        ),
        in_specs=[hbm] * 4,
        out_specs=(vmem,) * 4,
        scratch_shapes=[pltpu.VMEM(shape, dtype) for shape, dtype in scratch] + [
            dma((4,)), dma((6,)), dma((6,)),
            dma((2, tiles_n - 1)), dma((2, tiles_n)),
            dma((2, team - 1)), dma((2, team)),
        ],
        compiler_params=pltpu.CompilerParams(
            collective_id=0, has_side_effects=True, vmem_limit_bytes=24 * 2**20
        ),
        name="conv_step",
    )(*(pltpu.with_memory_space_constraint(a, pltpu.HBM) for a in (volumes[0], w1, w2, cotangent[0])))
    if q_y > 1:
        half = q_y * 108 // nz
        zl = lax.rem(lax.axis_index("space"), nz)
        grad_one = lax.dynamic_slice_in_dim(g1[:, :108].reshape(-1), zl * half, half, 0)
        return features[None], pooled_grad[None], grad_one, g2[:, :864].reshape(-1)
    features, pooled_grad, grad_one, grad_two = pl.pallas_call(
        finish,
        out_shape=(
            jax.ShapeDtypeStruct((64, 2, 256), BF16),
            jax.ShapeDtypeStruct((32, 2, 256), BF16),
            jax.ShapeDtypeStruct((54,), F32),
            jax.ShapeDtypeStruct((864,), F32),
        ),
        in_specs=[vmem] * 4,
        out_specs=(hbm,) * 4,
        scratch_shapes=[pltpu.VMEM((54,), F32), pltpu.VMEM((864,), F32), dma((4,))],
        compiler_params=pltpu.CompilerParams(vmem_limit_bytes=2 * 2**20),
        name="finish",
    )(features, pooled_grad, g1, g2)
    return features[None], pooled_grad[None], grad_one, grad_two


def solution(mesh):
    slabs, dp_n = mesh.shape["space"], mesh.shape["dp"]
    sizes = (4, 8, 2, dp_n) if slabs == 64 else (2, 2, slabs // 4, dp_n)
    in_specs = (P("dp", None, "space", None, None), P(), P(), P("dp", None, "space", None))
    out_specs = (P("dp", None, "space", None), P("dp", None, "space", None), P("space"), P("space"))
    return jax.shard_map(
        functools.partial(on_device, sizes), mesh=mesh, in_specs=in_specs, out_specs=out_specs,
        check_vma=False,
    )
```

```python
import functools
import math

import jax
import jax.numpy as jnp
from jax import lax
from jax.experimental import pallas as pl
from jax.experimental.pallas import tpu as pltpu
from jax.sharding import PartitionSpec as P

F32 = jnp.float32
BF16 = jnp.bfloat16
TAPS = [(a, b) for a in (-1, 0, 1) for b in (-1, 0, 1)]
NT = (((1,), (1,)), ((), ()))


def dot(a, b):
    return jnp.dot(a, b, preferred_element_type=F32)


def dot_nt(a, b):
    return lax.dot_general(a, b, NT, preferred_element_type=F32)


def iota(shape, dim):
    return lax.broadcasted_iota(jnp.int32, shape, dim)


def tap_masks(width):
    lane = iota((1, width * width), 1)
    row, col = lane // width, lane % width
    rows = {-1: row >= 1, 0: None, 1: row < width - 1}
    cols = {-1: col >= 1, 0: None, 1: col < width - 1}
    masks = []
    for dr, dc in TAPS:
        parts = [m for m in (rows[dr], cols[dc]) if m is not None]
        mask = None
        for part in parts:
            mask = part if mask is None else jnp.logical_and(mask, part)
        masks.append(mask)
    return masks


def shifted(block, tap, masks, width, sign=1):
    dr, dc = TAPS[tap]
    dr, dc = sign * dr, sign * dc
    if dr == 0 and dc == 0:
        return block
    size = width * width
    moved = pltpu.roll(block, (-(dr * width + dc)) % size, 1)
    return jnp.where(masks[TAPS.index((dr, dc))], moved, jnp.zeros_like(moved))


def one_hot(shape, column_of_row):
    return jnp.where(iota(shape, 1) == column_of_row(iota(shape, 0)), 1.0, 0.0).astype(BF16)


def silu_parts(half):
    t = jnp.tanh(half)
    return half + half * t, 0.5 + 0.5 * t


def kernel(
    sizes, cols,
    vol_in, w1_in, w2_in, cot_in,
    feat, pgrad, g1_out, g2_out,
    vol, w1, w2, cot,
    vrows, planes, cots, cotr, w1rows,
    x1, tsel, w1big, pool, dsilu_one, w2band, wp, place,
    xcol_a, xcol_b,
    g2s, g2x, g2z, g2r,
    g1s, g1x, g1z, g1r,
    local, halo_send, halo_recv, xs, xr, zs, zr, news,
):
    nx, ny, nz, dp_n = sizes
    slabs = nx * ny * nz
    space = lax.axis_index("space")
    dp = lax.axis_index("dp")
    zl = lax.rem(space, nz)
    xy = lax.div(space, nz)
    tiles_n = nx * ny
    nxt = lax.rem(space + 1, slabs)
    prv = lax.rem(space + slabs - 1, slabs)
    nxt2 = lax.rem(space + 2, slabs)
    prv2 = lax.rem(space + slabs - 2, slabs)
    team = nz * dp_n
    me_z = zl * dp_n + dp

    yi = lax.rem(xy, ny)
    xi = lax.div(xy, ny)
    core = lax.rem(dp, 2)
    ring_z = nz * dp_n // 2
    zi = lax.div(dp, 2) * nz + zl

    def at(dx, dy, dz, dc):
        ox, oy = lax.rem(xi + dx % nx, nx), lax.rem(yi + dy % ny, ny)
        oz, oc = lax.rem(zi + dz % ring_z, ring_z), lax.rem(core + dc, 2)
        return (ox * ny + oy) * nz + lax.rem(oz, nz), lax.div(oz, nz) * 2 + oc

    def around(d, n):
        return min(d, n - d)

    xy_offsets = sorted(
        ((dx, dy) for dx in range(nx) for dy in range(ny) if dx or dy),
        key=lambda o: -around(o[0], nx) - around(o[1], ny),
    )
    z_offsets = sorted(
        ((dz, dc) for dz in range(ring_z) for dc in range(2) if dz or dc),
        key=lambda o: -around(o[0], ring_z) - 0.5 * o[1],
    )

    def xy_peer(r):
        dx, dy = xy_offsets[r - 1]
        peer = at(dx, dy, 0, 0)
        return lax.div(peer[0], nz), peer

    def z_peer(r):
        dz, dc = z_offsets[r - 1]
        peer = at(0, 0, dz, dc)
        oz = lax.rem(peer[0], nz)
        return oz * dp_n + peer[1], oz, peer

    def signal(sem, where):
        for peer in where:
            pl.semaphore_signal(sem, inc=1, device_id=peer, device_id_type=pl.DeviceIdType.MESH)

    near = [at(0, 0, 0, 1)]
    near += [at(d, 0, 0, 0) for d in (-1, 1)] + [at(0, d, 0, 0) for d in (-1, 1)]
    near += [at(0, 0, d, 0) for d in (-1, 1)]
    wide = [at(2, 0, 0, 0)] if nx > 2 else []
    wide += [at(0, d, 0, 0) for d in (-2, 2)] if ny > 2 else []
    wide += [at(0, 0, d, 0) for d in (-2, 2)] if ring_z > 2 else []
    widest = ([at(0, d, 0, 0) for d in (-2, 2)] if ny > 2 else []) + [at(0, 0, 0, 1)]

    loads = [
        pltpu.make_async_copy(src, dst, local.at[i])
        for i, (src, dst) in enumerate([(vol_in, vol), (cot_in, cot), (w1_in, w1), (w2_in, w2)])
    ]
    for copy in loads:
        copy.start()
    barrier = pltpu.get_barrier_semaphore()
    entry = [(nxt, dp), (prv, dp), (nxt2, dp), (prv2, dp)] + near
    signal(barrier, entry)

    def send(src, dst, ssem, rsem, peer):
        copy = pltpu.make_async_remote_copy(
            src_ref=src, dst_ref=dst, send_sem=ssem, recv_sem=rsem,
            device_id=peer, device_id_type=pl.DeviceIdType.MESH,
        )
        copy.start()
        return copy

    loads[0].wait()
    for p in range(4):
        for c in range(4):
            vrows[(p * 4 + c) * 32:(p * 4 + c) * 32 + 32, :] = vol[c, p].astype(F32)
    own = jnp.concatenate(
        [
            jnp.concatenate([vrows[pl.ds(4 * j + k, 16, stride=32), :] for k in range(4)], axis=1)
            for j in range(8)
        ],
        axis=1,
    )
    planes[5:9] = own.astype(BF16).reshape(4, 4, 1024)
    planes[14:16] = jnp.zeros((2, 4, 1024), BF16)
    loads[1].wait()
    split = one_hot((128, 128), lambda r: (r % 64) * 2 + r // 64)
    merge = one_hot((128, 128), lambda r: (r % 2) * 64 + r // 2)
    merge_half = one_hot((64, 64), lambda r: (r % 2) * 32 + r // 2)
    own_cot = dot(split, cot[...].reshape(128, 256))
    cots[0] = own_cot[0:64].astype(BF16)
    cots[1] = own_cot[64:128].astype(BF16)

    pl.semaphore_wait(barrier, len(entry))
    halos = [
        send(planes.at[5:9], planes.at[1:5], halo_send.at[0], halo_recv.at[0], (nxt, dp)),
        send(planes.at[5:9], planes.at[9:13], halo_send.at[1], halo_recv.at[1], (prv, dp)),
        send(planes.at[8], planes.at[0], halo_send.at[2], halo_recv.at[2], (nxt2, dp)),
        send(planes.at[5], planes.at[13], halo_send.at[3], halo_recv.at[3], (prv2, dp)),
        send(cots.at[1], cotr.at[0], halo_send.at[4], halo_recv.at[4], (nxt, dp)),
        send(cots.at[0], cotr.at[1], halo_send.at[5], halo_recv.at[5], (prv, dp)),
    ]

    signal(news.at[0], near)

    k = iota((1, 224), 1)
    m = k % 48
    odd = jnp.logical_and(m >= 24, k < 192)
    v_k = (k // 48) * 2 + jnp.where(odd, 1, 0)
    p_k = jnp.where(odd, jnp.where(m < 32, m // 4 - 2, m // 4 - 8), m // 4)
    for d in range(4):
        kd = p_k - d
        ok = jnp.logical_and(kd >= 0, kd <= 2)
        target = jnp.where(ok, (k % 4) * 27 + kd * 9 + v_k, -1)
        tsel[d] = jnp.where(iota((128, 224), 0) == target, 1.0, 0.0).astype(BF16)
    w1rows[...] = jnp.zeros((128, 128), F32)
    loads[2].wait()
    for t in range(27):
        w1rows[pl.ds(t, 4, stride=27), 0:32] = w1[t].astype(F32)
    w1t = w1rows[...].T[0:32].astype(BF16)
    for d in range(4):
        w1big[d * 32:(d + 1) * 32, :] = (0.5 * dot(w1t, tsel[d])).astype(BF16)

    pl.semaphore_wait(news.at[0], len(near))
    signal(news.at[1], wide)
    for blk in range(4):
        r = iota((256, 256), 0) + blk * 256
        pool[blk * 256:(blk + 1) * 256, :] = jnp.where(
            iota((256, 256), 1) == (r // 64) * 16 + (r % 32) // 2, 1.0, 0.0
        ).astype(BF16)

    loads[3].wait()
    zero = jnp.zeros((32, 64), F32)
    for v in range(9):
        w = [w2[kd * 9 + v].astype(F32) for kd in range(3)]
        left = jnp.concatenate([w[0], w[1], w[2], zero], axis=0)
        right = jnp.concatenate([zero, w[0], w[1], w[2]], axis=0)
        both = jnp.concatenate([left, right], axis=1)
        w2band[:, v * 128:(v + 1) * 128] = (0.5 * both.T).astype(BF16)
        top = jnp.concatenate([w[2], w[1], w[0], zero], axis=1)
        bottom = jnp.concatenate([zero, w[2], w[1], w[0]], axis=1)
        wp[v * 64:v * 64 + 32, :] = top.astype(BF16)
        wp[v * 64 + 32:v * 64 + 64, :] = bottom.astype(BF16)

    if wide:
        pl.semaphore_wait(news.at[1], len(wide))
    signal(news.at[2], widest)
    for copy in halos[0:4]:
        copy.wait_recv()
    first, last = space == 0, space == slabs - 1
    row = iota((64, 1), 0) // 4
    inside = jnp.logical_and(row >= 5 - 4 * space, row < 5 + 4 * (slabs - space))
    field = jnp.where(inside, planes[...].reshape(64, 1024).astype(F32), 0.0).astype(BF16)
    masks_one = tap_masks(32)
    blocks = []
    for v in range(9):
        blocks.append(shifted(field, v, masks_one, 32))
        if v % 2 == 0 and v < 8:
            continue
        for g in range(3):
            top, mid, low = g * 16, g * 16 + 16, g * 16 + 24
            if v == 8:
                x1[g, 192:224, :] = blocks[8][top:top + 32]
                continue
            base = (v // 2) * 48
            x1[g, base:base + 16, :] = blocks[v - 1][top:mid]
            x1[g, base + 16:base + 32, :] = jnp.concatenate(
                [blocks[v - 1][mid:low], blocks[v][mid:low]], axis=0
            )
            x1[g, base + 32:base + 48, :] = blocks[v][top:mid]
    masks = tap_masks(16)
    for g in (0, 2, 1):
        sums = None
        for n in range(4):
            lanes = slice(n * 256, (n + 1) * 256)
            act, s = silu_parts(dot(w1big[...], x1[g, :, lanes]))
            if g == 1:
                dsilu_one[:, lanes] = s + act * (1.0 - s)
            total = jnp.concatenate([act[0:32] + act[32:64], act[64:96] + act[96:128]], axis=0)
            high = total.astype(BF16)
            low = (total - high.astype(F32)).astype(BF16)
            part = dot(jnp.concatenate([high, low], axis=0), pool[lanes, :])
            sums = part if sums is None else sums + part
        pooled = (sums[0:64] + sums[64:128]) * 0.125
        if g == 0:
            pooled = jnp.where(first, 0.0, pooled)
        if g == 2:
            pooled = jnp.where(last, 0.0, pooled)
        pooled = pooled.astype(BF16)
        for v in range(9):
            block = shifted(pooled, v, masks, 16)
            if g < 2:
                xcol_a[v * 128 + g * 64:v * 128 + g * 64 + 64, :] = block
            if g > 0:
                xcol_b[v * 128 + g * 64 - 64:v * 128 + g * 64, :] = block

    halos[4].wait_recv()
    halos[5].wait_recv()
    cot_a = jnp.concatenate([cotr[0].astype(F32), cots[0].astype(F32)], axis=0)
    cot_b = jnp.concatenate([cots[1].astype(F32), cotr[1].astype(F32)], axis=0)
    act_a, s_a = silu_parts(dot(w2band[...], xcol_a[...]))
    delta_a = cot_a * (s_a + act_a * (1.0 - s_a))
    act_b, s_b = silu_parts(dot(w2band[...], xcol_b[...]))
    delta_b = cot_b * (s_b + act_b * (1.0 - s_b))
    delta = jnp.concatenate(
        [
            jnp.where(first, 0.0, delta_a[0:64]),
            delta_a[64:128],
            delta_b[0:64],
            jnp.where(last, 0.0, delta_b[64:128]),
        ],
        axis=0,
    ).astype(BF16)

    rows_xy, rows_z = 64 // tiles_n, 64 // slabs
    scale_two = 1.0 / 512.0 * math.sqrt(64 * 8 / (slabs * dp_n))
    lower = dot_nt(delta[64:128], xcol_a[...])
    upper = dot_nt(delta[128:192], xcol_b[...])
    tiles = []
    for v in range(9):
        lanes = slice(v * 128, (v + 1) * 128)
        tiles.append(pltpu.roll(lower[:, lanes], 96, 1) + upper[:, lanes])
    lane = iota((1, 128), 1)
    for v in range(7):
        tile = tiles[v]
        if v < 6:
            kd = v % 3
            tile = jnp.where(lane < 96, tile, pltpu.roll(tiles[7 + v // 3], 96 - kd * 32, 1))
        g2s[:, :, v * 128:(v + 1) * 128] = (tile * scale_two).astype(BF16).reshape(tiles_n, rows_xy, 128)
    pl.semaphore_wait(news.at[2], len(widest))
    g2_x = []
    for r in range(1, tiles_n):
        other, peer = xy_peer(r)
        g2_x.append(send(g2s.at[other], g2x.at[xy], xs.at[0, r - 1], xr.at[0, xy], peer))
    for copy in halos:
        copy.wait_send()

    z = dot(wp[...], delta)
    total = None
    for v in range(9):
        term = shifted(z[v * 64:(v + 1) * 64], v, masks, 16, sign=-1)
        total = term if total is None else total + term
    pg = total.astype(BF16)

    g1k = None
    for n in range(4):
        lanes = slice(n * 256, (n + 1) * 256)
        spread = dot_nt(pg, pool[lanes, :]) * 0.125
        twice = jnp.concatenate([spread[0:32], spread[0:32], spread[32:64], spread[32:64]], axis=0)
        one = (twice * dsilu_one[:, lanes]).astype(BF16)
        part = dot_nt(one, x1[1, :, lanes])
        g1k = part if g1k is None else g1k + part
    hi = g1k.astype(BF16)
    mid = (g1k - hi.astype(F32)).astype(BF16)
    g1 = None
    for d in range(4):
        rows = slice(d * 32, (d + 1) * 32)
        out = dot_nt(jnp.concatenate([hi[rows], mid[rows]], axis=0), tsel[d])
        g1 = out if g1 is None else g1 + out
    g1 = (g1[0:32] + g1[32:64]) * (1.0 / math.sqrt(4096 * slabs * dp_n))
    q_y = 32 // tiles_n
    g1s[...] = g1.reshape(tiles_n, q_y, 128)
    g1_x = []
    for r in range(1, tiles_n):
        other, peer = xy_peer(r)
        g1_x.append(send(g1s.at[other], g1x.at[xy], xs.at[1, r - 1], xr.at[1, xy], peer))
    g2x[xy] = g2s[xy]
    g1x[xy] = g1s[xy]

    own_feat = jnp.concatenate([act_a[64:128], act_b[0:64]], axis=0).astype(BF16)
    feat[...] = dot(merge, own_feat).astype(BF16).reshape(64, 2, 256)
    pgrad[...] = dot(merge_half, pg).astype(BF16).reshape(32, 2, 256)

    f = iota((1, 896), 1)
    f_v, f_kd, f_c = f % 9, (f % 27) // 9, f // 27
    f_row = jnp.where(f_v < 7, f_v, (f_v - 7) * 3 + f_kd)
    f_lane = jnp.where(f < 864, jnp.where(f_v < 7, f_kd * 32 + f_c, 96 + f_c), -1)
    place[...] = jnp.where(iota((128, 896), 0) == f_lane, 1.0, 0.0).astype(BF16)

    for r in range(1, tiles_n):
        other, peer = xy_peer(r)
        g2_x[r - 1].wait_send()
        pltpu.make_async_remote_copy(
            src_ref=g2s.at[xy], dst_ref=g2x.at[other], send_sem=xs.at[0, r - 1],
            recv_sem=xr.at[0, other], device_id=peer, device_id_type=pl.DeviceIdType.MESH,
        ).wait_recv()
    parts = g2x[...].reshape(64, cols).astype(F32)
    step = 64
    while step > max(rows_xy, 8):
        step //= 2
        parts = parts[0:step] + parts[step:2 * step]
    total = parts[0:rows_xy]
    for i in range(1, step // rows_xy):
        total = total + parts[i * rows_xy:(i + 1) * rows_xy]
    for i in range(nz):
        rows = []
        for q in range(i * rows_z, (i + 1) * rows_z):
            rows += [total[q:q + 1, v * 128:(v + 1) * 128] for v in range(7)] + [jnp.zeros((1, 128), F32)]
        g2z[i] = jnp.concatenate(rows, axis=0).astype(BF16)
    g2r[me_z] = g2z[zl]
    g2_z = []
    for r in range(1, team):
        other, oz, peer = z_peer(r)
        g2_z.append(send(g2z.at[oz], g2r.at[me_z], zs.at[0, r - 1], zr.at[0, me_z], peer))

    for r in range(1, tiles_n):
        other, peer = xy_peer(r)
        g1_x[r - 1].wait_send()
        pltpu.make_async_remote_copy(
            src_ref=g1s.at[xy], dst_ref=g1x.at[other], send_sem=xs.at[1, r - 1],
            recv_sem=xr.at[1, other], device_id=peer, device_id_type=pl.DeviceIdType.MESH,
        ).wait_recv()
    parts = g1x[...].reshape(32, 128)
    step = 32
    while step > max(q_y, 8):
        step //= 2
        parts = parts[0:step] + parts[step:2 * step]
    total = parts[0:q_y]
    for i in range(1, step // q_y):
        total = total + parts[i * q_y:(i + 1) * q_y]
    g1z[...] = total
    g1r[me_z] = total
    g1_z = []
    for r in range(1, team):
        other, oz, peer = z_peer(r)
        g1_z.append(send(g1z, g1r.at[me_z], zs.at[1, r - 1], zr.at[1, me_z], peer))

    for r in range(1, team):
        other, oz, peer = z_peer(r)
        g2_z[r - 1].wait_send()
        pltpu.make_async_remote_copy(
            src_ref=g2z.at[zl], dst_ref=g2r.at[other], send_sem=zs.at[0, r - 1],
            recv_sem=zr.at[0, other], device_id=peer, device_id_type=pl.DeviceIdType.MESH,
        ).wait_recv()
    total = g2r[0].astype(F32)
    for r in range(1, team):
        total = total + g2r[r].astype(F32)
    for q in range(rows_z):
        packed = total[q * 8:q * 8 + 8]
        hi = packed.astype(BF16)
        rest = packed - hi.astype(F32)
        mid = rest.astype(BF16)
        low = (rest - mid.astype(F32)).astype(BF16)
        split3 = jnp.concatenate([hi.astype(F32), mid.astype(F32), low.astype(F32)], axis=0)
        spread = dot(split3.astype(BF16), place[...])
        spread = spread[0:8] + (spread[8:16] + spread[16:24])
        spread = jnp.where(iota((8, 896), 0) == f_row, spread, 0.0)
        g2_out[q:q + 1, :] = jnp.sum(spread, axis=0, keepdims=True)
    for r in range(1, team):
        other, oz, peer = z_peer(r)
        g1_z[r - 1].wait_send()
        pltpu.make_async_remote_copy(
            src_ref=g1z, dst_ref=g1r.at[other], send_sem=zs.at[1, r - 1],
            recv_sem=zr.at[1, other], device_id=peer, device_id_type=pl.DeviceIdType.MESH,
        ).wait_recv()
    total = g1r[0]
    for r in range(1, team):
        total = total + g1r[r]
    if q_y == 1:
        total = jnp.where(zl == 0, total, pltpu.roll(total, 128 - 54, 1))
    g1_out[...] = total


def finish(feat, pgrad, g1, g2, feat_out, pgrad_out, g1_out, g2_out, one, two, sems):
    copies = [
        pltpu.make_async_copy(feat, feat_out, sems.at[0]),
        pltpu.make_async_copy(pgrad, pgrad_out, sems.at[1]),
    ]
    for copy in copies:
        copy.start()
    one[...] = g1[0, 0:54]
    two[...] = g2[0, 0:864]
    tails = [
        pltpu.make_async_copy(one, g1_out, sems.at[2]),
        pltpu.make_async_copy(two, g2_out, sems.at[3]),
    ]
    for copy in tails:
        copy.start()
    for copy in copies + tails:
        copy.wait()


def on_device(sizes, volumes, kernel_one, kernel_two, cotangent):
    nx, ny, nz, dp_n = sizes
    slabs, team = nx * ny * nz, nz * dp_n
    w1 = jnp.transpose(kernel_one, (2, 3, 4, 1, 0)).reshape(27, 4, 32)
    w2 = jnp.transpose(kernel_two, (2, 3, 4, 1, 0)).reshape(27, 32, 64)
    tiles_n = nx * ny
    rows_xy, rows_z, q_y = 64 // tiles_n, 64 // slabs, 32 // tiles_n
    cols = 896
    vmem = pl.BlockSpec(memory_space=pltpu.VMEM)
    hbm = pl.BlockSpec(memory_space=pltpu.HBM)
    scratch = [
        ((4, 4, 32, 32), BF16),
        ((27, 4, 32), BF16),
        ((27, 32, 64), BF16),
        ((64, 2, 256), BF16),
        ((512, 32), F32),
        ((16, 4, 1024), BF16),
        ((2, 64, 256), BF16),
        ((2, 64, 256), BF16),
        ((128, 128), F32),
        ((3, 224, 1024), BF16),
        ((4, 128, 224), BF16),
        ((128, 224), BF16),
        ((1024, 256), BF16),
        ((128, 1024), F32),
        ((128, 1152), BF16),
        ((576, 256), BF16),
        ((128, cols), BF16),
        ((1152, 256), BF16),
        ((1152, 256), BF16),
        ((tiles_n, rows_xy, cols), BF16),
        ((tiles_n, rows_xy, cols), BF16),
        ((nz, rows_z * 8, 128), BF16),
        ((team, rows_z * 8, 128), BF16),
        ((tiles_n, q_y, 128), F32),
        ((tiles_n, q_y, 128), F32),
        ((q_y, 128), F32),
        ((team, q_y, 128), F32),
    ]
    dma = pltpu.SemaphoreType.DMA
    features, pooled_grad, g1, g2 = pl.pallas_call(
        functools.partial(kernel, sizes, cols),
        out_shape=(
            jax.ShapeDtypeStruct((64, 2, 256), BF16),
            jax.ShapeDtypeStruct((32, 2, 256), BF16),
            jax.ShapeDtypeStruct((q_y, 128), F32),
            jax.ShapeDtypeStruct((rows_z, cols), F32),
        ),
        in_specs=[hbm] * 4,
        out_specs=(vmem,) * 4,
        scratch_shapes=[pltpu.VMEM(shape, dtype) for shape, dtype in scratch] + [
            dma((4,)), dma((6,)), dma((6,)),
            dma((2, tiles_n - 1)), dma((2, tiles_n)),
            dma((2, team - 1)), dma((2, team)),
            pltpu.SemaphoreType.REGULAR((3,)),
        ],
        compiler_params=pltpu.CompilerParams(
            collective_id=0, has_side_effects=True, vmem_limit_bytes=24 * 2**20
        ),
        name="conv_step",
    )(*(pltpu.with_memory_space_constraint(a, pltpu.HBM) for a in (volumes[0], w1, w2, cotangent[0])))
    if q_y > 1:
        half = q_y * 108 // nz
        zl = lax.rem(lax.axis_index("space"), nz)
        grad_one = lax.dynamic_slice_in_dim(g1[:, :108].reshape(-1), zl * half, half, 0)
        return features[None], pooled_grad[None], grad_one, g2[:, :864].reshape(-1)
    features, pooled_grad, grad_one, grad_two = pl.pallas_call(
        finish,
        out_shape=(
            jax.ShapeDtypeStruct((64, 2, 256), BF16),
            jax.ShapeDtypeStruct((32, 2, 256), BF16),
            jax.ShapeDtypeStruct((54,), F32),
            jax.ShapeDtypeStruct((864,), F32),
        ),
        in_specs=[vmem] * 4,
        out_specs=(hbm,) * 4,
        scratch_shapes=[pltpu.VMEM((54,), F32), pltpu.VMEM((864,), F32), dma((4,))],
        compiler_params=pltpu.CompilerParams(vmem_limit_bytes=2 * 2**20),
        name="finish",
    )(features, pooled_grad, g1, g2)
    return features[None], pooled_grad[None], grad_one, grad_two


def solution(mesh):
    slabs, dp_n = mesh.shape["space"], mesh.shape["dp"]
    sizes = (4, 8, 2, dp_n) if slabs == 64 else (2, 2, slabs // 4, dp_n)
    in_specs = (P("dp", None, "space", None, None), P(), P(), P("dp", None, "space", None))
    out_specs = (P("dp", None, "space", None), P("dp", None, "space", None), P("space"), P("space"))
    return jax.shard_map(
        functools.partial(on_device, sizes), mesh=mesh, in_specs=in_specs, out_specs=out_specs,
        check_vma=False,
    )
```

```python
import functools
import math

import jax
import jax.numpy as jnp
from jax import lax
from jax.experimental import pallas as pl
from jax.experimental.pallas import tpu as pltpu
from jax.sharding import PartitionSpec as P

F32 = jnp.float32
BF16 = jnp.bfloat16
TAPS = [(a, b) for a in (-1, 0, 1) for b in (-1, 0, 1)]
NT = (((1,), (1,)), ((), ()))


def dot(a, b):
    return jnp.dot(a, b, preferred_element_type=F32)


def dot_nt(a, b):
    return lax.dot_general(a, b, NT, preferred_element_type=F32)


def iota(shape, dim):
    return lax.broadcasted_iota(jnp.int32, shape, dim)


def tap_masks(width):
    lane = iota((1, width * width), 1)
    row, col = lane // width, lane % width
    rows = {-1: row >= 1, 0: None, 1: row < width - 1}
    cols = {-1: col >= 1, 0: None, 1: col < width - 1}
    masks = []
    for dr, dc in TAPS:
        parts = [m for m in (rows[dr], cols[dc]) if m is not None]
        mask = None
        for part in parts:
            mask = part if mask is None else jnp.logical_and(mask, part)
        masks.append(mask)
    return masks


def shifted(block, tap, masks, width, sign=1):
    dr, dc = TAPS[tap]
    dr, dc = sign * dr, sign * dc
    if dr == 0 and dc == 0:
        return block
    size = width * width
    moved = pltpu.roll(block, (-(dr * width + dc)) % size, 1)
    return jnp.where(masks[TAPS.index((dr, dc))], moved, jnp.zeros_like(moved))


def one_hot(shape, column_of_row):
    return jnp.where(iota(shape, 1) == column_of_row(iota(shape, 0)), 1.0, 0.0).astype(BF16)


def silu_parts(half):
    t = jnp.tanh(half)
    return half + half * t, 0.5 + 0.5 * t


def kernel(
    sizes, cols,
    vol_in, w1_in, w2_in, cot_in,
    feat, pgrad, g1_out, g2_out,
    vol, w1, w2, cot,
    vrows, planes, cots, cotr, w1rows,
    x1, tsel, w1big, pool, dsilu_one, w2band, wp, place,
    xcol_a, xcol_b,
    g2s, g2x, g1s, g1x, gz, gr,
    local, halo_send, halo_recv, xs, xr, zs, zr, news,
):
    nx, ny, nz, dp_n = sizes
    slabs = nx * ny * nz
    space = lax.axis_index("space")
    dp = lax.axis_index("dp")
    zl = lax.rem(space, nz)
    xy = lax.div(space, nz)
    tiles_n = nx * ny
    nxt = lax.rem(space + 1, slabs)
    prv = lax.rem(space + slabs - 1, slabs)
    nxt2 = lax.rem(space + 2, slabs)
    prv2 = lax.rem(space + slabs - 2, slabs)
    team = nz * dp_n
    me_z = zl * dp_n + dp

    yi = lax.rem(xy, ny)
    xi = lax.div(xy, ny)
    core = lax.rem(dp, 2)
    ring_z = nz * dp_n // 2
    zi = lax.div(dp, 2) * nz + zl

    def at(dx, dy, dz, dc):
        ox, oy = lax.rem(xi + dx % nx, nx), lax.rem(yi + dy % ny, ny)
        oz, oc = lax.rem(zi + dz % ring_z, ring_z), lax.rem(core + dc, 2)
        return (ox * ny + oy) * nz + lax.rem(oz, nz), lax.div(oz, nz) * 2 + oc

    def around(d, n):
        return min(d, n - d)

    xy_offsets = sorted(
        ((dx, dy) for dx in range(nx) for dy in range(ny) if dx or dy),
        key=lambda o: -around(o[0], nx) - around(o[1], ny),
    )
    z_offsets = sorted(
        ((dz, dc) for dz in range(ring_z) for dc in range(2) if dz or dc),
        key=lambda o: -around(o[0], ring_z) - 0.5 * o[1],
    )

    def xy_peer(r):
        dx, dy = xy_offsets[r - 1]
        peer = at(dx, dy, 0, 0)
        return lax.div(peer[0], nz), peer

    def z_peer(r):
        dz, dc = z_offsets[r - 1]
        peer = at(0, 0, dz, dc)
        oz = lax.rem(peer[0], nz)
        return oz * dp_n + peer[1], oz, peer

    def signal(sem, where):
        for peer in where:
            pl.semaphore_signal(sem, inc=1, device_id=peer, device_id_type=pl.DeviceIdType.MESH)

    near = [at(0, 0, 0, 1)]
    near += [at(d, 0, 0, 0) for d in range(1, nx)]
    near += [at(0, d, 0, 0) for d in (-2, -1, 1, 2) if ny > 2 or abs(d) == 1]
    near += [at(0, 0, d, 0) for d in (-2, -1, 1, 2) if ring_z > 2 or abs(d) == 1]
    wide = [at(d, 0, 0, 0) for d in range(1, nx)] + [at(0, 0, 0, 1)]

    barrier = pltpu.get_barrier_semaphore()
    loads = [
        pltpu.make_async_copy(src, dst, local.at[i])
        for i, (src, dst) in enumerate([(vol_in, vol), (cot_in, cot), (w1_in, w1), (w2_in, w2)])
    ]
    for copy in loads:
        copy.start()
    entry = [(nxt, dp), (prv, dp), (nxt2, dp), (prv2, dp)] + near
    signal(barrier, entry)

    def send(src, dst, ssem, rsem, peer):
        copy = pltpu.make_async_remote_copy(
            src_ref=src, dst_ref=dst, send_sem=ssem, recv_sem=rsem,
            device_id=peer, device_id_type=pl.DeviceIdType.MESH,
        )
        copy.start()
        return copy

    loads[0].wait()
    for p in range(4):
        for c in range(4):
            vrows[(p * 4 + c) * 32:(p * 4 + c) * 32 + 32, :] = vol[c, p].astype(F32)
    own = jnp.concatenate(
        [
            jnp.concatenate([vrows[pl.ds(4 * j + k, 16, stride=32), :] for k in range(4)], axis=1)
            for j in range(8)
        ],
        axis=1,
    )
    planes[5:9] = own.astype(BF16).reshape(4, 4, 1024)
    planes[14:16] = jnp.zeros((2, 4, 1024), BF16)
    loads[1].wait()
    split = one_hot((128, 128), lambda r: (r % 64) * 2 + r // 64)
    merge = one_hot((128, 128), lambda r: (r % 2) * 64 + r // 2)
    merge_half = one_hot((64, 64), lambda r: (r % 2) * 32 + r // 2)
    own_cot = dot(split, cot[...].reshape(128, 256))
    cots[0] = own_cot[0:64].astype(BF16)
    cots[1] = own_cot[64:128].astype(BF16)

    pl.semaphore_wait(barrier, len(entry))
    halos = [
        send(planes.at[5:9], planes.at[1:5], halo_send.at[0], halo_recv.at[0], (nxt, dp)),
        send(planes.at[5:9], planes.at[9:13], halo_send.at[1], halo_recv.at[1], (prv, dp)),
        send(planes.at[8], planes.at[0], halo_send.at[2], halo_recv.at[2], (nxt2, dp)),
        send(planes.at[5], planes.at[13], halo_send.at[3], halo_recv.at[3], (prv2, dp)),
        send(cots.at[1], cotr.at[0], halo_send.at[4], halo_recv.at[4], (nxt, dp)),
        send(cots.at[0], cotr.at[1], halo_send.at[5], halo_recv.at[5], (prv, dp)),
    ]

    signal(news.at[0], near)

    k = iota((1, 224), 1)
    m = k % 48
    odd = jnp.logical_and(m >= 24, k < 192)
    v_k = (k // 48) * 2 + jnp.where(odd, 1, 0)
    p_k = jnp.where(odd, jnp.where(m < 32, m // 4 - 2, m // 4 - 8), m // 4)
    for d in range(4):
        kd = p_k - d
        ok = jnp.logical_and(kd >= 0, kd <= 2)
        target = jnp.where(ok, (k % 4) * 27 + kd * 9 + v_k, -1)
        tsel[d] = jnp.where(iota((128, 224), 0) == target, 1.0, 0.0).astype(BF16)
    w1rows[...] = jnp.zeros((128, 128), F32)
    loads[2].wait()
    for t in range(27):
        w1rows[pl.ds(t, 4, stride=27), 0:32] = w1[t].astype(F32)
    w1t = w1rows[...].T[0:32].astype(BF16)
    for d in range(4):
        w1big[d * 32:(d + 1) * 32, :] = (0.5 * dot(w1t, tsel[d])).astype(BF16)

    pl.semaphore_wait(news.at[0], len(near))
    signal(news.at[1], wide)
    for blk in range(4):
        r = iota((256, 256), 0) + blk * 256
        pool[blk * 256:(blk + 1) * 256, :] = jnp.where(
            iota((256, 256), 1) == (r // 64) * 16 + (r % 32) // 2, 1.0, 0.0
        ).astype(BF16)

    loads[3].wait()
    zero = jnp.zeros((32, 64), F32)
    for v in range(9):
        w = [w2[kd * 9 + v].astype(F32) for kd in range(3)]
        left = jnp.concatenate([w[0], w[1], w[2], zero], axis=0)
        right = jnp.concatenate([zero, w[0], w[1], w[2]], axis=0)
        both = jnp.concatenate([left, right], axis=1)
        w2band[:, v * 128:(v + 1) * 128] = (0.5 * both.T).astype(BF16)
        top = jnp.concatenate([w[2], w[1], w[0], zero], axis=1)
        bottom = jnp.concatenate([zero, w[2], w[1], w[0]], axis=1)
        wp[v * 64:v * 64 + 32, :] = top.astype(BF16)
        wp[v * 64 + 32:v * 64 + 64, :] = bottom.astype(BF16)

    for copy in halos[0:4]:
        copy.wait_recv()
    first, last = space == 0, space == slabs - 1
    row = iota((64, 1), 0) // 4
    inside = jnp.logical_and(row >= 5 - 4 * space, row < 5 + 4 * (slabs - space))
    field = jnp.where(inside, planes[...].reshape(64, 1024).astype(F32), 0.0).astype(BF16)
    masks_one = tap_masks(32)
    blocks = []
    for v in range(9):
        blocks.append(shifted(field, v, masks_one, 32))
        if v % 2 == 0 and v < 8:
            continue
        for g in range(3):
            top, mid, low = g * 16, g * 16 + 16, g * 16 + 24
            if v == 8:
                x1[g, 192:224, :] = blocks[8][top:top + 32]
                continue
            base = (v // 2) * 48
            x1[g, base:base + 16, :] = blocks[v - 1][top:mid]
            x1[g, base + 16:base + 32, :] = jnp.concatenate(
                [blocks[v - 1][mid:low], blocks[v][mid:low]], axis=0
            )
            x1[g, base + 32:base + 48, :] = blocks[v][top:mid]
    masks = tap_masks(16)
    for g in (0, 2, 1):
        sums = None
        for n in range(4):
            lanes = slice(n * 256, (n + 1) * 256)
            act, s = silu_parts(dot(w1big[...], x1[g, :, lanes]))
            if g == 1:
                dsilu_one[:, lanes] = s + act * (1.0 - s)
            total = jnp.concatenate([act[0:32] + act[32:64], act[64:96] + act[96:128]], axis=0)
            high = total.astype(BF16)
            low = (total - high.astype(F32)).astype(BF16)
            part = dot(jnp.concatenate([high, low], axis=0), pool[lanes, :])
            sums = part if sums is None else sums + part
        pooled = (sums[0:64] + sums[64:128]) * 0.125
        if g == 0:
            pooled = jnp.where(first, 0.0, pooled)
        if g == 2:
            pooled = jnp.where(last, 0.0, pooled)
        pooled = pooled.astype(BF16)
        for v in range(9):
            block = shifted(pooled, v, masks, 16)
            if g < 2:
                xcol_a[v * 128 + g * 64:v * 128 + g * 64 + 64, :] = block
            if g > 0:
                xcol_b[v * 128 + g * 64 - 64:v * 128 + g * 64, :] = block

    halos[4].wait_recv()
    halos[5].wait_recv()
    cot_a = jnp.concatenate([cotr[0].astype(F32), cots[0].astype(F32)], axis=0)
    cot_b = jnp.concatenate([cots[1].astype(F32), cotr[1].astype(F32)], axis=0)
    act_a, s_a = silu_parts(dot(w2band[...], xcol_a[...]))
    delta_a = cot_a * (s_a + act_a * (1.0 - s_a))
    act_b, s_b = silu_parts(dot(w2band[...], xcol_b[...]))
    delta_b = cot_b * (s_b + act_b * (1.0 - s_b))
    delta = jnp.concatenate(
        [
            jnp.where(first, 0.0, delta_a[0:64]),
            delta_a[64:128],
            delta_b[0:64],
            jnp.where(last, 0.0, delta_b[64:128]),
        ],
        axis=0,
    ).astype(BF16)

    rows_xy, rows_z = 64 // tiles_n, 64 // slabs
    scale_two = 1.0 / 512.0 * math.sqrt(64 * 8 / (slabs * dp_n))
    lower = dot_nt(delta[64:128], xcol_a[...])
    upper = dot_nt(delta[128:192], xcol_b[...])
    tiles = []
    for v in range(9):
        lanes = slice(v * 128, (v + 1) * 128)
        tiles.append(pltpu.roll(lower[:, lanes], 96, 1) + upper[:, lanes])
    lane = iota((1, 128), 1)
    for v in range(7):
        tile = tiles[v]
        if v < 6:
            kd = v % 3
            tile = jnp.where(lane < 96, tile, pltpu.roll(tiles[7 + v // 3], 96 - kd * 32, 1))
        g2s[:, :, v * 128:(v + 1) * 128] = (tile * scale_two).astype(BF16).reshape(tiles_n, rows_xy, 128)
    pl.semaphore_wait(news.at[1], len(wide))
    for r in range(1, tiles_n):
        other, peer = xy_peer(r)
        send(g2s.at[other], g2x.at[xy], xs.at[0], xr.at[0], peer)
    for copy in halos:
        copy.wait_send()

    z = dot(wp[...], delta)
    total = None
    for v in range(9):
        term = shifted(z[v * 64:(v + 1) * 64], v, masks, 16, sign=-1)
        total = term if total is None else total + term
    pg = total.astype(BF16)

    g1k = None
    for n in range(4):
        lanes = slice(n * 256, (n + 1) * 256)
        spread = dot_nt(pg, pool[lanes, :]) * 0.125
        twice = jnp.concatenate([spread[0:32], spread[0:32], spread[32:64], spread[32:64]], axis=0)
        one = (twice * dsilu_one[:, lanes]).astype(BF16)
        part = dot_nt(one, x1[1, :, lanes])
        g1k = part if g1k is None else g1k + part
    hi = g1k.astype(BF16)
    mid = (g1k - hi.astype(F32)).astype(BF16)
    g1 = None
    for d in range(4):
        rows = slice(d * 32, (d + 1) * 32)
        out = dot_nt(jnp.concatenate([hi[rows], mid[rows]], axis=0), tsel[d])
        g1 = out if g1 is None else g1 + out
    g1 = (g1[0:32] + g1[32:64]) * (1.0 / math.sqrt(4096 * slabs * dp_n))
    q_y = 32 // tiles_n
    g1s[...] = g1.reshape(tiles_n, q_y, 128)
    for r in range(1, tiles_n):
        other, peer = xy_peer(r)
        send(g1s.at[other], g1x.at[xy], xs.at[1], xr.at[1], peer)
    g2x[xy] = g2s[xy]
    g1x[xy] = g1s[xy]

    own_feat = jnp.concatenate([act_a[64:128], act_b[0:64]], axis=0).astype(BF16)
    feat[...] = dot(merge, own_feat).astype(BF16).reshape(64, 2, 256)
    pgrad[...] = dot(merge_half, pg).astype(BF16).reshape(32, 2, 256)

    f = iota((1, 896), 1)
    f_v, f_kd, f_c = f % 9, (f % 27) // 9, f // 27
    f_row = jnp.where(f_v < 7, f_v, (f_v - 7) * 3 + f_kd)
    f_lane = jnp.where(f < 864, jnp.where(f_v < 7, f_kd * 32 + f_c, 96 + f_c), -1)
    place[...] = jnp.where(iota((128, 896), 0) == f_lane, 1.0, 0.0).astype(BF16)

    def whole(src, dst, count, ssem, rsem):
        return pltpu.make_async_remote_copy(
            src_ref=src.at[0:count], dst_ref=dst.at[0:count], send_sem=ssem, recv_sem=rsem,
            device_id=at(1, 0, 0, 0), device_id_type=pl.DeviceIdType.MESH,
        )

    def fold(parts, rows):
        step = parts.shape[0]
        while step > max(rows, 8):
            step //= 2
            parts = parts[0:step] + parts[step:2 * step]
        total = parts[0:rows]
        for i in range(1, step // rows):
            total = total + parts[i * rows:(i + 1) * rows]
        return total

    all_two = whole(g2s, g2x, tiles_n - 1, xs.at[0], xr.at[0])
    all_one = whole(g1s, g1x, tiles_n - 1, xs.at[1], xr.at[1])
    all_two.wait_recv()
    sum_two = fold(g2x[...].reshape(64, cols).astype(F32), rows_xy)
    all_one.wait_recv()
    sum_one = fold(g1x[...].reshape(32, 128), q_y)
    for i in range(nz):
        rows = []
        for q in range(rows_z):
            at_row = slice(i * rows_z + q, i * rows_z + q + 1)
            rows += [sum_two[at_row, v * 128:(v + 1) * 128] for v in range(7)] + [sum_one[q:q + 1]]
        gz[i] = jnp.concatenate(rows, axis=0).astype(BF16)
    for r in range(1, team):
        other, oz, peer = z_peer(r)
        send(gz.at[oz], gr.at[me_z], zs.at[0], zr.at[0], peer)
    gr[me_z] = gz[zl]
    all_two.wait_send()
    all_one.wait_send()
    pltpu.make_async_remote_copy(
        src_ref=gr.at[0:team - 1], dst_ref=gr.at[0:team - 1], send_sem=zs.at[0], recv_sem=zr.at[0],
        device_id=at(1, 0, 0, 0), device_id_type=pl.DeviceIdType.MESH,
    ).wait()
    total = gr[0].astype(F32)
    for r in range(1, team):
        total = total + gr[r].astype(F32)
    for q in range(rows_z):
        packed = total[q * 8:q * 8 + 8]
        hi = packed.astype(BF16)
        rest = packed - hi.astype(F32)
        mid = rest.astype(BF16)
        low = (rest - mid.astype(F32)).astype(BF16)
        split3 = jnp.concatenate([hi.astype(F32), mid.astype(F32), low.astype(F32)], axis=0)
        spread = dot(split3.astype(BF16), place[...])
        spread = spread[0:8] + (spread[8:16] + spread[16:24])
        spread = jnp.where(iota((8, 896), 0) == f_row, spread, 0.0)
        g2_out[q:q + 1, :] = jnp.sum(spread, axis=0, keepdims=True)
        one = packed[7:8]
        if rows_z == 1:
            one = jnp.where(zl == 0, one, pltpu.roll(one, 128 - 54, 1))
        g1_out[q:q + 1, :] = one


def finish(feat, pgrad, g1, g2, feat_out, pgrad_out, g1_out, g2_out, one, two, sems):
    copies = [
        pltpu.make_async_copy(feat, feat_out, sems.at[0]),
        pltpu.make_async_copy(pgrad, pgrad_out, sems.at[1]),
    ]
    for copy in copies:
        copy.start()
    one[...] = g1[0, 0:54]
    two[...] = g2[0, 0:864]
    tails = [
        pltpu.make_async_copy(one, g1_out, sems.at[2]),
        pltpu.make_async_copy(two, g2_out, sems.at[3]),
    ]
    for copy in tails:
        copy.start()
    for copy in copies + tails:
        copy.wait()


def on_device(sizes, volumes, kernel_one, kernel_two, cotangent):
    nx, ny, nz, dp_n = sizes
    slabs, team = nx * ny * nz, nz * dp_n
    w1 = jnp.transpose(kernel_one, (2, 3, 4, 1, 0)).reshape(27, 4, 32)
    w2 = jnp.transpose(kernel_two, (2, 3, 4, 1, 0)).reshape(27, 32, 64)
    tiles_n = nx * ny
    rows_xy, rows_z, q_y = 64 // tiles_n, 64 // slabs, 32 // tiles_n
    cols = 896
    vmem = pl.BlockSpec(memory_space=pltpu.VMEM)
    hbm = pl.BlockSpec(memory_space=pltpu.HBM)
    scratch = [
        ((4, 4, 32, 32), BF16),
        ((27, 4, 32), BF16),
        ((27, 32, 64), BF16),
        ((64, 2, 256), BF16),
        ((512, 32), F32),
        ((16, 4, 1024), BF16),
        ((2, 64, 256), BF16),
        ((2, 64, 256), BF16),
        ((128, 128), F32),
        ((3, 224, 1024), BF16),
        ((4, 128, 224), BF16),
        ((128, 224), BF16),
        ((1024, 256), BF16),
        ((128, 1024), F32),
        ((128, 1152), BF16),
        ((576, 256), BF16),
        ((128, cols), BF16),
        ((1152, 256), BF16),
        ((1152, 256), BF16),
        ((tiles_n, rows_xy, cols), BF16),
        ((tiles_n, rows_xy, cols), BF16),
        ((tiles_n, q_y, 128), F32),
        ((tiles_n, q_y, 128), F32),
        ((nz, rows_z * 8, 128), BF16),
        ((team, rows_z * 8, 128), BF16),
    ]
    dma = pltpu.SemaphoreType.DMA
    features, pooled_grad, g1, g2 = pl.pallas_call(
        functools.partial(kernel, sizes, cols),
        out_shape=(
            jax.ShapeDtypeStruct((64, 2, 256), BF16),
            jax.ShapeDtypeStruct((32, 2, 256), BF16),
            jax.ShapeDtypeStruct((q_y, 128), F32),
            jax.ShapeDtypeStruct((rows_z, cols), F32),
        ),
        in_specs=[hbm] * 4,
        out_specs=(vmem,) * 4,
        scratch_shapes=[pltpu.VMEM(shape, dtype) for shape, dtype in scratch] + [
            dma((4,)), dma((6,)), dma((6,)),
            dma((2,)), dma((2,)), dma((1,)), dma((1,)),
            pltpu.SemaphoreType.REGULAR((2,)),
        ],
        compiler_params=pltpu.CompilerParams(
            collective_id=0, has_side_effects=True, vmem_limit_bytes=24 * 2**20
        ),
        name="conv_step",
    )(*(pltpu.with_memory_space_constraint(a, pltpu.HBM) for a in (volumes[0], w1, w2, cotangent[0])))
    if q_y > 1:
        half = q_y * 108 // nz
        zl = lax.rem(lax.axis_index("space"), nz)
        grad_one = lax.dynamic_slice_in_dim(g1[:, :108].reshape(-1), zl * half, half, 0)
        return features[None], pooled_grad[None], grad_one, g2[:, :864].reshape(-1)
    features, pooled_grad, grad_one, grad_two = pl.pallas_call(
        finish,
        out_shape=(
            jax.ShapeDtypeStruct((64, 2, 256), BF16),
            jax.ShapeDtypeStruct((32, 2, 256), BF16),
            jax.ShapeDtypeStruct((54,), F32),
            jax.ShapeDtypeStruct((864,), F32),
        ),
        in_specs=[vmem] * 4,
        out_specs=(hbm,) * 4,
        scratch_shapes=[pltpu.VMEM((54,), F32), pltpu.VMEM((864,), F32), dma((4,))],
        compiler_params=pltpu.CompilerParams(vmem_limit_bytes=2 * 2**20),
        name="finish",
    )(features, pooled_grad, g1, g2)
    return features[None], pooled_grad[None], grad_one, grad_two


def solution(mesh):
    slabs, dp_n = mesh.shape["space"], mesh.shape["dp"]
    sizes = (4, 8, 2, dp_n) if slabs == 64 else (2, 2, slabs // 4, dp_n)
    in_specs = (P("dp", None, "space", None, None), P(), P(), P("dp", None, "space", None))
    out_specs = (P("dp", None, "space", None), P("dp", None, "space", None), P("space"), P("space"))
    return jax.shard_map(
        functools.partial(on_device, sizes), mesh=mesh, in_specs=in_specs, out_specs=out_specs,
        check_vma=False,
    )
```

```python
import functools
import math

import jax
import jax.numpy as jnp
from jax import lax
from jax.experimental import pallas as pl
from jax.experimental.pallas import tpu as pltpu
from jax.sharding import PartitionSpec as P

F32 = jnp.float32
BF16 = jnp.bfloat16
TAPS = [(a, b) for a in (-1, 0, 1) for b in (-1, 0, 1)]
NT = (((1,), (1,)), ((), ()))


def dot(a, b):
    return jnp.dot(a, b, preferred_element_type=F32)


def dot_nt(a, b):
    return lax.dot_general(a, b, NT, preferred_element_type=F32)


def iota(shape, dim):
    return lax.broadcasted_iota(jnp.int32, shape, dim)


def tap_masks(width):
    lane = iota((1, width * width), 1)
    row, col = lane // width, lane % width
    rows = {-1: row >= 1, 0: None, 1: row < width - 1}
    cols = {-1: col >= 1, 0: None, 1: col < width - 1}
    masks = []
    for dr, dc in TAPS:
        parts = [m for m in (rows[dr], cols[dc]) if m is not None]
        mask = None
        for part in parts:
            mask = part if mask is None else jnp.logical_and(mask, part)
        masks.append(mask)
    return masks


def shifted(block, tap, masks, width, sign=1):
    dr, dc = TAPS[tap]
    dr, dc = sign * dr, sign * dc
    if dr == 0 and dc == 0:
        return block
    size = width * width
    moved = pltpu.roll(block, (-(dr * width + dc)) % size, 1)
    return jnp.where(masks[TAPS.index((dr, dc))], moved, jnp.zeros_like(moved))


def one_hot(shape, column_of_row):
    return jnp.where(iota(shape, 1) == column_of_row(iota(shape, 0)), 1.0, 0.0).astype(BF16)


def shifted_bf16(block, tap, mask, width):
    dr, dc = TAPS[tap]
    if dr == 0 and dc == 0:
        return block
    moved = pltpu.roll(block, (-(dr * width + dc)) % (width * width), 1)
    return jnp.concatenate(
        [moved[r:r + 16] * mask for r in range(0, block.shape[0], 16)], axis=0
    )


def silu_parts(half):
    t = jnp.tanh(half)
    return half + half * t, 0.5 + 0.5 * t


def kernel(
    sizes, cols,
    vol_in, w1_in, w2_in, cot_in,
    feat, pgrad, g1_out, g2_out,
    vol, w1, w2, cot,
    vrows, planes, cots, cotr, w1rows,
    ones_one, ones_two, x1, tsel, w1big, pool, dsilu_one, w2band, wp, place,
    xcol_a, xcol_b, xcol_c,
    g2s, g2x, g1s, g1x, gz, gr,
    local, halo_send, halo_recv, xs, xr, zs, zr, news,
):
    nx, ny, nz, dp_n = sizes
    slabs = nx * ny * nz
    space = lax.axis_index("space")
    dp = lax.axis_index("dp")
    zl = lax.rem(space, nz)
    xy = lax.div(space, nz)
    tiles_n = nx * ny
    nxt = lax.rem(space + 1, slabs)
    prv = lax.rem(space + slabs - 1, slabs)
    nxt2 = lax.rem(space + 2, slabs)
    prv2 = lax.rem(space + slabs - 2, slabs)
    team = nz * dp_n
    me_z = zl * dp_n + dp

    yi = lax.rem(xy, ny)
    xi = lax.div(xy, ny)
    core = lax.rem(dp, 2)
    ring_z = nz * dp_n // 2
    zi = lax.div(dp, 2) * nz + zl

    def at(dx, dy, dz, dc):
        ox, oy = lax.rem(xi + dx % nx, nx), lax.rem(yi + dy % ny, ny)
        oz, oc = lax.rem(zi + dz % ring_z, ring_z), lax.rem(core + dc, 2)
        return (ox * ny + oy) * nz + lax.rem(oz, nz), lax.div(oz, nz) * 2 + oc

    def around(d, n):
        return min(d, n - d)

    xy_offsets = sorted(
        ((dx, dy) for dx in range(nx) for dy in range(ny) if dx or dy),
        key=lambda o: -around(o[0], nx) - around(o[1], ny),
    )
    z_offsets = sorted(
        ((dz, dc) for dz in range(ring_z) for dc in range(2) if dz or dc),
        key=lambda o: -around(o[0], ring_z) - 0.5 * o[1],
    )

    def xy_peer(r):
        dx, dy = xy_offsets[r - 1]
        peer = at(dx, dy, 0, 0)
        return lax.div(peer[0], nz), peer

    def z_peer(r):
        dz, dc = z_offsets[r - 1]
        peer = at(0, 0, dz, dc)
        oz = lax.rem(peer[0], nz)
        return oz * dp_n + peer[1], oz, peer

    def signal(sem, where):
        for peer in where:
            pl.semaphore_signal(sem, inc=1, device_id=peer, device_id_type=pl.DeviceIdType.MESH)

    near = [at(0, 0, 0, 1)]
    near += [at(d, 0, 0, 0) for d in range(1, nx)]
    near += [at(0, d, 0, 0) for d in (-2, -1, 1, 2) if ny > 2 or abs(d) == 1]
    near += [at(0, 0, d, 0) for d in (-2, -1, 1, 2) if ring_z > 2 or abs(d) == 1]
    wide = [at(d, 0, 0, 0) for d in range(1, nx)] + [at(0, 0, 0, 1)]

    barrier = pltpu.get_barrier_semaphore()
    loads = [
        pltpu.make_async_copy(src, dst, local.at[i])
        for i, (src, dst) in enumerate([(vol_in, vol), (cot_in, cot), (w1_in, w1), (w2_in, w2)])
    ]
    for copy in loads:
        copy.start()
    entry = [(nxt, dp), (prv, dp), (nxt2, dp), (prv2, dp)] + near
    signal(barrier, entry)

    def send(src, dst, ssem, rsem, peer):
        copy = pltpu.make_async_remote_copy(
            src_ref=src, dst_ref=dst, send_sem=ssem, recv_sem=rsem,
            device_id=peer, device_id_type=pl.DeviceIdType.MESH,
        )
        copy.start()
        return copy

    loads[0].wait()
    for p in range(4):
        for c in range(4):
            vrows[(p * 4 + c) * 32:(p * 4 + c) * 32 + 32, :] = vol[c, p].astype(F32)
    own = jnp.concatenate(
        [
            jnp.concatenate([vrows[pl.ds(4 * j + k, 16, stride=32), :] for k in range(4)], axis=1)
            for j in range(8)
        ],
        axis=1,
    )
    planes[5:9] = own.astype(BF16).reshape(4, 4, 1024)
    planes[14:16] = jnp.zeros((2, 4, 1024), BF16)
    pl.semaphore_wait(barrier, len(entry))
    halos = [
        send(planes.at[5:9], planes.at[1:5], halo_send.at[0], halo_recv.at[0], (nxt, dp)),
        send(planes.at[5:9], planes.at[9:13], halo_send.at[1], halo_recv.at[1], (prv, dp)),
        send(planes.at[8], planes.at[0], halo_send.at[2], halo_recv.at[2], (nxt2, dp)),
        send(planes.at[5], planes.at[13], halo_send.at[3], halo_recv.at[3], (prv2, dp)),
    ]

    signal(news.at[0], near)
    loads[1].wait()
    split = one_hot((128, 128), lambda r: (r % 64) * 2 + r // 64)
    merge = one_hot((128, 128), lambda r: (r % 2) * 64 + r // 2)
    merge_half = one_hot((64, 64), lambda r: (r % 2) * 32 + r // 2)
    own_cot = dot(split, cot[...].reshape(128, 256))
    cots[0] = own_cot[0:64].astype(BF16)
    cots[1] = own_cot[64:128].astype(BF16)
    halos += [
        send(cots.at[1], cotr.at[0], halo_send.at[4], halo_recv.at[4], (nxt, dp)),
        send(cots.at[0], cotr.at[1], halo_send.at[5], halo_recv.at[5], (prv, dp)),
    ]

    k = iota((1, 224), 1)
    m = k % 48
    odd = jnp.logical_and(m >= 24, k < 192)
    v_k = (k // 48) * 2 + jnp.where(odd, 1, 0)
    p_k = jnp.where(odd, jnp.where(m < 32, m // 4 - 2, m // 4 - 8), m // 4)
    for d in range(4):
        kd = p_k - d
        ok = jnp.logical_and(kd >= 0, kd <= 2)
        target = jnp.where(ok, (k % 4) * 27 + kd * 9 + v_k, -1)
        tsel[d] = jnp.where(iota((128, 224), 0) == target, 1.0, 0.0).astype(BF16)
    w1rows[...] = jnp.zeros((128, 128), F32)
    loads[2].wait()
    for t in range(27):
        w1rows[pl.ds(t, 4, stride=27), 0:32] = w1[t].astype(F32)
    w1t = w1rows[...].T[0:32].astype(BF16)
    for d in range(4):
        w1big[d * 32:(d + 1) * 32, :] = (0.5 * dot(w1t, tsel[d])).astype(BF16)

    pl.semaphore_wait(news.at[0], len(near))
    signal(news.at[1], wide)
    for blk in range(4):
        r = iota((256, 256), 0) + blk * 256
        pool[blk * 256:(blk + 1) * 256, :] = jnp.where(
            iota((256, 256), 1) == (r // 64) * 16 + (r % 32) // 2, 1.0, 0.0
        ).astype(BF16)

    for ones, width in ((ones_one, 32), (ones_two, 16)):
        for v, mask in enumerate(tap_masks(width)):
            if mask is not None:
                row = jnp.where(mask, 1.0, 0.0)
                ones[v] = jnp.broadcast_to(row, (16, width * width)).astype(BF16)
    loads[3].wait()
    zero = jnp.zeros((32, 64), F32)
    for v in range(9):
        w = [w2[kd * 9 + v].astype(F32) for kd in range(3)]
        left = jnp.concatenate([w[0], w[1], w[2], zero], axis=0)
        right = jnp.concatenate([zero, w[0], w[1], w[2]], axis=0)
        both = jnp.concatenate([left, right], axis=1)
        w2band[:, v * 128:(v + 1) * 128] = (0.5 * both.T).astype(BF16)
        top = jnp.concatenate([w[2], w[1], w[0], zero], axis=1)
        bottom = jnp.concatenate([zero, w[2], w[1], w[0]], axis=1)
        wp[v * 64:v * 64 + 32, :] = top.astype(BF16)
        wp[v * 64 + 32:v * 64 + 64, :] = bottom.astype(BF16)

    for copy in halos[0:4]:
        copy.wait_recv()
    first, last = space == 0, space == slabs - 1
    row = iota((64, 1), 0) // 4
    inside = jnp.logical_and(row >= 5 - 4 * space, row < 5 + 4 * (slabs - space))
    field = jnp.where(inside, planes[...].reshape(64, 1024).astype(F32), 0.0).astype(BF16)
    blocks = []
    for v in range(9):
        blocks.append(shifted_bf16(field, v, ones_one[v], 32))
        if v % 2 == 0 and v < 8:
            continue
        for g in range(3):
            top, mid, low = g * 16, g * 16 + 16, g * 16 + 24
            if v == 8:
                x1[g, 192:224, :] = blocks[8][top:top + 32]
                continue
            base = (v // 2) * 48
            x1[g, base:base + 16, :] = blocks[v - 1][top:mid]
            x1[g, base + 16:base + 32, :] = jnp.concatenate(
                [blocks[v - 1][mid:low], blocks[v][mid:low]], axis=0
            )
            x1[g, base + 32:base + 48, :] = blocks[v][top:mid]
    masks = tap_masks(16)
    for g in (0, 2, 1):
        sums = None
        for n in range(4):
            lanes = slice(n * 256, (n + 1) * 256)
            act, s = silu_parts(dot(w1big[...], x1[g, :, lanes]))
            if g == 1:
                dsilu_one[:, lanes] = s + act * (1.0 - s)
            total = jnp.concatenate([act[0:32] + act[32:64], act[64:96] + act[96:128]], axis=0)
            high = total.astype(BF16)
            low = (total - high.astype(F32)).astype(BF16)
            part = dot(jnp.concatenate([high, low], axis=0), pool[lanes, :])
            sums = part if sums is None else sums + part
        pooled = (sums[0:64] + sums[64:128]) * 0.125
        if g == 0:
            pooled = jnp.where(first, 0.0, pooled)
        if g == 2:
            pooled = jnp.where(last, 0.0, pooled)
        pooled = pooled.astype(BF16)
        for v in range(9):
            block = shifted_bf16(pooled, v, ones_two[v], 16)
            if g == 0:
                xcol_c[v * 128:v * 128 + 32, :] = block[32:64]
            if g == 1:
                xcol_c[v * 128 + 32:v * 128 + 96, :] = block
            if g == 2:
                xcol_c[v * 128 + 96:v * 128 + 128, :] = block[0:32]
            if g < 2:
                xcol_a[v * 128 + g * 64:v * 128 + g * 64 + 64, :] = block
            if g > 0:
                xcol_b[v * 128 + g * 64 - 64:v * 128 + g * 64, :] = block

    halos[4].wait_recv()
    halos[5].wait_recv()
    cot_a = jnp.concatenate([cotr[0].astype(F32), cots[0].astype(F32)], axis=0)
    cot_b = jnp.concatenate([cots[1].astype(F32), cotr[1].astype(F32)], axis=0)
    act_a, s_a = silu_parts(dot(w2band[...], xcol_a[...]))
    delta_a = cot_a * (s_a + act_a * (1.0 - s_a))
    act_b, s_b = silu_parts(dot(w2band[...], xcol_b[...]))
    delta_b = cot_b * (s_b + act_b * (1.0 - s_b))
    delta = jnp.concatenate(
        [
            jnp.where(first, 0.0, delta_a[0:64]),
            delta_a[64:128],
            delta_b[0:64],
            jnp.where(last, 0.0, delta_b[64:128]),
        ],
        axis=0,
    ).astype(BF16)

    rows_xy, rows_z = 64 // tiles_n, 64 // slabs
    scale_two = 1.0 / 512.0 * math.sqrt(64 * 8 / (slabs * dp_n))
    outer = dot_nt(delta[64:192], xcol_c[...])
    tiles = []
    for v in range(9):
        lanes = slice(v * 128, (v + 1) * 128)
        tiles.append(outer[0:64, lanes] + pltpu.roll(outer[64:128, lanes], 96, 1))
    lane = iota((1, 128), 1)
    for v in range(7):
        tile = tiles[v]
        if v < 6:
            kd = v % 3
            tile = jnp.where(lane < 96, tile, pltpu.roll(tiles[7 + v // 3], 96 - kd * 32, 1))
        g2s[:, :, v * 128:(v + 1) * 128] = (tile * scale_two).astype(BF16).reshape(tiles_n, rows_xy, 128)
    pl.semaphore_wait(news.at[1], len(wide))
    for r in range(1, tiles_n):
        other, peer = xy_peer(r)
        send(g2s.at[other], g2x.at[xy], xs.at[0], xr.at[0], peer)
    z = dot(wp[...], delta)
    total = None
    for v in range(9):
        term = shifted(z[v * 64:(v + 1) * 64], v, masks, 16, sign=-1)
        total = term if total is None else total + term
    pg = total.astype(BF16)

    for copy in halos:
        copy.wait_send()

    g1k = None
    for n in range(4):
        lanes = slice(n * 256, (n + 1) * 256)
        spread = dot_nt(pg, pool[lanes, :]) * 0.125
        twice = jnp.concatenate([spread[0:32], spread[0:32], spread[32:64], spread[32:64]], axis=0)
        one = (twice * dsilu_one[:, lanes]).astype(BF16)
        part = dot_nt(one, x1[1, :, lanes])
        g1k = part if g1k is None else g1k + part
    hi = g1k.astype(BF16)
    mid = (g1k - hi.astype(F32)).astype(BF16)
    g1 = None
    for d in range(4):
        rows = slice(d * 32, (d + 1) * 32)
        out = dot_nt(jnp.concatenate([hi[rows], mid[rows]], axis=0), tsel[d])
        g1 = out if g1 is None else g1 + out
    g1 = (g1[0:32] + g1[32:64]) * (1.0 / math.sqrt(4096 * slabs * dp_n))
    q_y = 32 // tiles_n
    g1s[...] = g1.reshape(tiles_n, q_y, 128)
    for r in range(1, tiles_n):
        other, peer = xy_peer(r)
        send(g1s.at[other], g1x.at[xy], xs.at[1], xr.at[1], peer)
    g2x[xy] = g2s[xy]
    g1x[xy] = g1s[xy]

    own_feat = jnp.concatenate([act_a[64:128], act_b[0:64]], axis=0).astype(BF16)
    feat[...] = dot(merge, own_feat).astype(BF16).reshape(64, 2, 256)
    pgrad[...] = dot(merge_half, pg).astype(BF16).reshape(32, 2, 256)

    f = iota((1, 896), 1)
    f_v, f_kd, f_c = f % 9, (f % 27) // 9, f // 27
    f_row = jnp.where(f_v < 7, f_v, (f_v - 7) * 3 + f_kd)
    f_lane = jnp.where(f < 864, jnp.where(f_v < 7, f_kd * 32 + f_c, 96 + f_c), -1)
    place[...] = jnp.where(iota((128, 896), 0) == f_lane, 1.0, 0.0).astype(BF16)

    def whole(src, dst, count, ssem, rsem):
        return pltpu.make_async_remote_copy(
            src_ref=src.at[0:count], dst_ref=dst.at[0:count], send_sem=ssem, recv_sem=rsem,
            device_id=at(1, 0, 0, 0), device_id_type=pl.DeviceIdType.MESH,
        )

    def fold(parts, rows):
        step = parts.shape[0]
        while step > max(rows, 8):
            step //= 2
            parts = parts[0:step] + parts[step:2 * step]
        total = parts[0:rows]
        for i in range(1, step // rows):
            total = total + parts[i * rows:(i + 1) * rows]
        return total

    all_two = whole(g2s, g2x, tiles_n - 1, xs.at[0], xr.at[0])
    all_one = whole(g1s, g1x, tiles_n - 1, xs.at[1], xr.at[1])
    all_two.wait_recv()
    sum_two = fold(g2x[...].reshape(64, cols).astype(F32), rows_xy)
    all_one.wait_recv()
    sum_one = fold(g1x[...].reshape(32, 128), q_y)
    for i in range(nz):
        rows = []
        for q in range(rows_z):
            at_row = slice(i * rows_z + q, i * rows_z + q + 1)
            rows += [sum_two[at_row, v * 128:(v + 1) * 128] for v in range(7)] + [sum_one[q:q + 1]]
        gz[i] = jnp.concatenate(rows, axis=0).astype(BF16)
    for r in range(1, team):
        other, oz, peer = z_peer(r)
        send(gz.at[oz], gr.at[me_z], zs.at[0], zr.at[0], peer)
    gr[me_z] = gz[zl]
    all_two.wait_send()
    all_one.wait_send()
    pltpu.make_async_remote_copy(
        src_ref=gr.at[0:team - 1], dst_ref=gr.at[0:team - 1], send_sem=zs.at[0], recv_sem=zr.at[0],
        device_id=at(1, 0, 0, 0), device_id_type=pl.DeviceIdType.MESH,
    ).wait()
    total = gr[0].astype(F32)
    for r in range(1, team):
        total = total + gr[r].astype(F32)
    for q in range(rows_z):
        packed = total[q * 8:q * 8 + 8]
        hi = packed.astype(BF16)
        rest = packed - hi.astype(F32)
        mid = rest.astype(BF16)
        low = (rest - mid.astype(F32)).astype(BF16)
        split3 = jnp.concatenate([hi.astype(F32), mid.astype(F32), low.astype(F32)], axis=0)
        spread = dot(split3.astype(BF16), place[...])
        spread = spread[0:8] + (spread[8:16] + spread[16:24])
        spread = jnp.where(iota((8, 896), 0) == f_row, spread, 0.0)
        g2_out[q:q + 1, :] = jnp.sum(spread, axis=0, keepdims=True)
        one = packed[7:8]
        if rows_z == 1:
            one = jnp.where(zl == 0, one, pltpu.roll(one, 128 - 54, 1))
        g1_out[q:q + 1, :] = one


def finish(feat, pgrad, g1, g2, feat_out, pgrad_out, g1_out, g2_out, one, two, sems):
    copies = [
        pltpu.make_async_copy(feat, feat_out, sems.at[0]),
        pltpu.make_async_copy(pgrad, pgrad_out, sems.at[1]),
    ]
    for copy in copies:
        copy.start()
    one[...] = g1[0, 0:54]
    two[...] = g2[0, 0:864]
    tails = [
        pltpu.make_async_copy(one, g1_out, sems.at[2]),
        pltpu.make_async_copy(two, g2_out, sems.at[3]),
    ]
    for copy in tails:
        copy.start()
    for copy in copies + tails:
        copy.wait()


def on_device(sizes, volumes, kernel_one, kernel_two, cotangent):
    nx, ny, nz, dp_n = sizes
    slabs, team = nx * ny * nz, nz * dp_n
    w1 = jnp.transpose(kernel_one, (2, 3, 4, 1, 0)).reshape(27, 4, 32)
    w2 = jnp.transpose(kernel_two, (2, 3, 4, 1, 0)).reshape(27, 32, 64)
    tiles_n = nx * ny
    rows_xy, rows_z, q_y = 64 // tiles_n, 64 // slabs, 32 // tiles_n
    cols = 896
    vmem = pl.BlockSpec(memory_space=pltpu.VMEM)
    hbm = pl.BlockSpec(memory_space=pltpu.HBM)
    scratch = [
        ((4, 4, 32, 32), BF16),
        ((27, 4, 32), BF16),
        ((27, 32, 64), BF16),
        ((64, 2, 256), BF16),
        ((512, 32), F32),
        ((16, 4, 1024), BF16),
        ((2, 64, 256), BF16),
        ((2, 64, 256), BF16),
        ((128, 128), F32),
        ((9, 16, 1024), BF16),
        ((9, 16, 256), BF16),
        ((3, 224, 1024), BF16),
        ((4, 128, 224), BF16),
        ((128, 224), BF16),
        ((1024, 256), BF16),
        ((128, 1024), F32),
        ((128, 1152), BF16),
        ((576, 256), BF16),
        ((128, cols), BF16),
        ((1152, 256), BF16),
        ((1152, 256), BF16),
        ((1152, 256), BF16),
        ((tiles_n, rows_xy, cols), BF16),
        ((tiles_n, rows_xy, cols), BF16),
        ((tiles_n, q_y, 128), F32),
        ((tiles_n, q_y, 128), F32),
        ((nz, rows_z * 8, 128), BF16),
        ((team, rows_z * 8, 128), BF16),
    ]
    dma = pltpu.SemaphoreType.DMA
    features, pooled_grad, g1, g2 = pl.pallas_call(
        functools.partial(kernel, sizes, cols),
        out_shape=(
            jax.ShapeDtypeStruct((64, 2, 256), BF16),
            jax.ShapeDtypeStruct((32, 2, 256), BF16),
            jax.ShapeDtypeStruct((q_y, 128), F32),
            jax.ShapeDtypeStruct((rows_z, cols), F32),
        ),
        in_specs=[hbm] * 4,
        out_specs=(vmem,) * 4,
        scratch_shapes=[pltpu.VMEM(shape, dtype) for shape, dtype in scratch] + [
            dma((4,)), dma((6,)), dma((6,)),
            dma((2,)), dma((2,)), dma((1,)), dma((1,)),
            pltpu.SemaphoreType.REGULAR((2,)),
        ],
        compiler_params=pltpu.CompilerParams(
            collective_id=0, has_side_effects=True, vmem_limit_bytes=24 * 2**20
        ),
        name="conv_step",
    )(*(pltpu.with_memory_space_constraint(a, pltpu.HBM) for a in (volumes[0], w1, w2, cotangent[0])))
    if q_y > 1:
        half = q_y * 108 // nz
        zl = lax.rem(lax.axis_index("space"), nz)
        grad_one = lax.dynamic_slice_in_dim(g1[:, :108].reshape(-1), zl * half, half, 0)
        return features[None], pooled_grad[None], grad_one, g2[:, :864].reshape(-1)
    features, pooled_grad, grad_one, grad_two = pl.pallas_call(
        finish,
        out_shape=(
            jax.ShapeDtypeStruct((64, 2, 256), BF16),
            jax.ShapeDtypeStruct((32, 2, 256), BF16),
            jax.ShapeDtypeStruct((54,), F32),
            jax.ShapeDtypeStruct((864,), F32),
        ),
        in_specs=[vmem] * 4,
        out_specs=(hbm,) * 4,
        scratch_shapes=[pltpu.VMEM((54,), F32), pltpu.VMEM((864,), F32), dma((4,))],
        compiler_params=pltpu.CompilerParams(vmem_limit_bytes=2 * 2**20),
        name="finish",
    )(features, pooled_grad, g1, g2)
    return features[None], pooled_grad[None], grad_one, grad_two


def solution(mesh):
    slabs, dp_n = mesh.shape["space"], mesh.shape["dp"]
    sizes = (4, 8, 2, dp_n) if slabs == 64 else (2, 2, slabs // 4, dp_n)
    in_specs = (P("dp", None, "space", None, None), P(), P(), P("dp", None, "space", None))
    out_specs = (P("dp", None, "space", None), P("dp", None, "space", None), P("space"), P("space"))
    return jax.shard_map(
        functools.partial(on_device, sizes), mesh=mesh, in_specs=in_specs, out_specs=out_specs,
        check_vma=False,
    )
```

```python
import functools
import math

import jax
import jax.numpy as jnp
from jax import lax
from jax.experimental import pallas as pl
from jax.experimental.pallas import tpu as pltpu
from jax.sharding import PartitionSpec as P

F32 = jnp.float32
BF16 = jnp.bfloat16
TAPS = [(a, b) for a in (-1, 0, 1) for b in (-1, 0, 1)]
NT = (((1,), (1,)), ((), ()))


def dot(a, b):
    return jnp.dot(a, b, preferred_element_type=F32)


def dot_nt(a, b):
    return lax.dot_general(a, b, NT, preferred_element_type=F32)


def iota(shape, dim):
    return lax.broadcasted_iota(jnp.int32, shape, dim)


def tap_masks(width):
    lane = iota((1, width * width), 1)
    row, col = lane // width, lane % width
    rows = {-1: row >= 1, 0: None, 1: row < width - 1}
    cols = {-1: col >= 1, 0: None, 1: col < width - 1}
    masks = []
    for dr, dc in TAPS:
        parts = [m for m in (rows[dr], cols[dc]) if m is not None]
        mask = None
        for part in parts:
            mask = part if mask is None else jnp.logical_and(mask, part)
        masks.append(mask)
    return masks


def shifted(block, tap, masks, width, sign=1):
    dr, dc = TAPS[tap]
    dr, dc = sign * dr, sign * dc
    if dr == 0 and dc == 0:
        return block
    size = width * width
    moved = pltpu.roll(block, (-(dr * width + dc)) % size, 1)
    return jnp.where(masks[TAPS.index((dr, dc))], moved, jnp.zeros_like(moved))


def one_hot(shape, column_of_row):
    return jnp.where(iota(shape, 1) == column_of_row(iota(shape, 0)), 1.0, 0.0).astype(BF16)


def shifted_bf16(block, tap, mask, width):
    dr, dc = TAPS[tap]
    if dr == 0 and dc == 0:
        return block
    moved = pltpu.roll(block, (-(dr * width + dc)) % (width * width), 1)
    return jnp.concatenate(
        [moved[r:r + 16] * mask for r in range(0, block.shape[0], 16)], axis=0
    )


def silu_parts(half):
    t = jnp.tanh(half)
    return half + half * t, 0.5 + 0.5 * t


def kernel(
    sizes, cols,
    vol_in, w1_in, w2_in, cot_in,
    feat, pgrad, g1_out, g2_out,
    vol, w1, w2, cot,
    vrows, planes, cots, cotr, w1rows,
    ones_one, ones_two, x1, tsel, w1big, pool, dsilu_one, w2band, wp, place,
    xcol_a, xcol_b, xcol_c,
    g2s, g2x, g1s, g1x, gz, gr,
    local, halo_send, halo_recv, xs, xr, zs, zr, news,
):
    nx, ny, nz, dp_n = sizes
    slabs = nx * ny * nz
    space = lax.axis_index("space")
    dp = lax.axis_index("dp")
    zl = lax.rem(space, nz)
    xy = lax.div(space, nz)
    tiles_n = nx * ny
    nxt = lax.rem(space + 1, slabs)
    prv = lax.rem(space + slabs - 1, slabs)
    nxt2 = lax.rem(space + 2, slabs)
    prv2 = lax.rem(space + slabs - 2, slabs)
    team = nz * dp_n
    me_z = zl * dp_n + dp

    yi = lax.rem(xy, ny)
    xi = lax.div(xy, ny)
    core = lax.rem(dp, 2)
    ring_z = nz * dp_n // 2
    zi = lax.div(dp, 2) * nz + zl

    def at(dx, dy, dz, dc):
        ox, oy = lax.rem(xi + dx % nx, nx), lax.rem(yi + dy % ny, ny)
        oz, oc = lax.rem(zi + dz % ring_z, ring_z), lax.rem(core + dc, 2)
        return (ox * ny + oy) * nz + lax.rem(oz, nz), lax.div(oz, nz) * 2 + oc

    def around(d, n):
        return min(d, n - d)

    xy_offsets = sorted(
        ((dx, dy) for dx in range(nx) for dy in range(ny) if dx or dy),
        key=lambda o: -around(o[0], nx) - around(o[1], ny),
    )
    z_offsets = sorted(
        ((dz, dc) for dz in range(ring_z) for dc in range(2) if dz or dc),
        key=lambda o: -around(o[0], ring_z) - 0.5 * o[1],
    )

    def xy_peer(r):
        dx, dy = xy_offsets[r - 1]
        peer = at(dx, dy, 0, 0)
        return lax.div(peer[0], nz), peer

    def z_peer(r):
        dz, dc = z_offsets[r - 1]
        peer = at(0, 0, dz, dc)
        oz = lax.rem(peer[0], nz)
        return oz * dp_n + peer[1], oz, peer

    def signal(sem, where):
        for peer in where:
            pl.semaphore_signal(sem, inc=1, device_id=peer, device_id_type=pl.DeviceIdType.MESH)

    near = [at(0, 0, 0, 1)]
    near += [at(d, 0, 0, 0) for d in range(1, nx)]
    near += [at(0, d, 0, 0) for d in (-2, -1, 1, 2) if ny > 2 or abs(d) == 1]
    near += [at(0, 0, d, 0) for d in (-2, -1, 1, 2) if ring_z > 2 or abs(d) == 1]
    wide = [at(d, 0, 0, 0) for d in range(1, nx)] + [at(0, 0, 0, 1)]

    barrier = pltpu.get_barrier_semaphore()
    loads = [
        pltpu.make_async_copy(src, dst, local.at[i])
        for i, (src, dst) in enumerate([(vol_in, vol), (cot_in, cot), (w1_in, w1), (w2_in, w2)])
    ]
    for copy in loads:
        copy.start()
    entry = [(nxt, dp), (prv, dp), (nxt2, dp), (prv2, dp)] + near
    signal(barrier, entry)

    def send(src, dst, ssem, rsem, peer):
        copy = pltpu.make_async_remote_copy(
            src_ref=src, dst_ref=dst, send_sem=ssem, recv_sem=rsem,
            device_id=peer, device_id_type=pl.DeviceIdType.MESH,
        )
        copy.start()
        return copy

    loads[0].wait()
    for p in range(4):
        for c in range(4):
            vrows[(p * 4 + c) * 32:(p * 4 + c) * 32 + 32, :] = vol[c, p].astype(F32)
    own = jnp.concatenate(
        [
            jnp.concatenate([vrows[pl.ds(4 * j + k, 16, stride=32), :] for k in range(4)], axis=1)
            for j in range(8)
        ],
        axis=1,
    )
    planes[5:9] = own.astype(BF16).reshape(4, 4, 1024)
    planes[14:16] = jnp.zeros((2, 4, 1024), BF16)
    pl.semaphore_wait(barrier, len(entry))
    halos = [
        send(planes.at[5:9], planes.at[1:5], halo_send.at[0], halo_recv.at[0], (nxt, dp)),
        send(planes.at[5:9], planes.at[9:13], halo_send.at[1], halo_recv.at[1], (prv, dp)),
        send(planes.at[8], planes.at[0], halo_send.at[2], halo_recv.at[2], (nxt2, dp)),
        send(planes.at[5], planes.at[13], halo_send.at[3], halo_recv.at[3], (prv2, dp)),
    ]

    signal(news.at[0], near)
    loads[1].wait()
    split = one_hot((128, 128), lambda r: (r % 64) * 2 + r // 64)
    merge = one_hot((128, 128), lambda r: (r % 2) * 64 + r // 2)
    merge_half = one_hot((64, 64), lambda r: (r % 2) * 32 + r // 2)
    own_cot = dot(split, cot[...].reshape(128, 256))
    cots[0] = own_cot[0:64].astype(BF16)
    cots[1] = own_cot[64:128].astype(BF16)
    halos += [
        send(cots.at[1], cotr.at[0], halo_send.at[4], halo_recv.at[4], (nxt, dp)),
        send(cots.at[0], cotr.at[1], halo_send.at[5], halo_recv.at[5], (prv, dp)),
    ]

    k = iota((1, 224), 1)
    m = k % 48
    odd = jnp.logical_and(m >= 24, k < 192)
    v_k = (k // 48) * 2 + jnp.where(odd, 1, 0)
    p_k = jnp.where(odd, jnp.where(m < 32, m // 4 - 2, m // 4 - 8), m // 4)
    for d in range(4):
        kd = p_k - d
        ok = jnp.logical_and(kd >= 0, kd <= 2)
        target = jnp.where(ok, (k % 4) * 27 + kd * 9 + v_k, -1)
        tsel[d] = jnp.where(iota((128, 224), 0) == target, 1.0, 0.0).astype(BF16)
    w1rows[...] = jnp.zeros((128, 128), F32)
    loads[2].wait()
    for t in range(27):
        w1rows[pl.ds(t, 4, stride=27), 0:32] = w1[t].astype(F32)
    w1t = w1rows[...].T[0:32].astype(BF16)
    for d in range(4):
        w1big[d * 32:(d + 1) * 32, :] = (0.5 * dot(w1t, tsel[d])).astype(BF16)

    pl.semaphore_wait(news.at[0], len(near))
    signal(news.at[1], wide)
    for blk in range(4):
        r = iota((256, 256), 0) + blk * 256
        pool[blk * 256:(blk + 1) * 256, :] = jnp.where(
            iota((256, 256), 1) == (r // 64) * 16 + (r % 32) // 2, 1.0, 0.0
        ).astype(BF16)

    for ones, width in ((ones_one, 32), (ones_two, 16)):
        for v, mask in enumerate(tap_masks(width)):
            if mask is not None:
                row = jnp.where(mask, 1.0, 0.0)
                ones[v] = jnp.broadcast_to(row, (16, width * width)).astype(BF16)
    loads[3].wait()
    zero = jnp.zeros((32, 64), F32)
    for v in range(9):
        w = [w2[kd * 9 + v].astype(F32) for kd in range(3)]
        left = jnp.concatenate([w[0], w[1], w[2], zero], axis=0)
        right = jnp.concatenate([zero, w[0], w[1], w[2]], axis=0)
        both = jnp.concatenate([left, right], axis=1)
        w2band[:, v * 128:(v + 1) * 128] = (0.5 * both.T).astype(BF16)
        top = jnp.concatenate([w[2], w[1], w[0], zero], axis=1)
        bottom = jnp.concatenate([zero, w[2], w[1], w[0]], axis=1)
        wp[v * 64:v * 64 + 32, :] = top.astype(BF16)
        wp[v * 64 + 32:v * 64 + 64, :] = bottom.astype(BF16)

    for copy in halos[0:4]:
        copy.wait_recv()
    first, last = space == 0, space == slabs - 1
    row = iota((64, 1), 0) // 4
    inside = jnp.logical_and(row >= 5 - 4 * space, row < 5 + 4 * (slabs - space))
    field = jnp.where(inside, planes[...].reshape(64, 1024).astype(F32), 0.0).astype(BF16)
    blocks = []
    for v in range(9):
        blocks.append(shifted_bf16(field, v, ones_one[v], 32))
        if v % 2 == 0 and v < 8:
            continue
        for g in range(3):
            top, mid, low = g * 16, g * 16 + 16, g * 16 + 24
            if v == 8:
                x1[g, 192:224, :] = blocks[8][top:top + 32]
                continue
            base = (v // 2) * 48
            x1[g, base:base + 16, :] = blocks[v - 1][top:mid]
            x1[g, base + 16:base + 32, :] = jnp.concatenate(
                [blocks[v - 1][mid:low], blocks[v][mid:low]], axis=0
            )
            x1[g, base + 32:base + 48, :] = blocks[v][top:mid]
    masks = tap_masks(16)
    for g in (0, 2, 1):
        sums = None
        for n in range(4):
            lanes = slice(n * 256, (n + 1) * 256)
            act, s = silu_parts(dot(w1big[...], x1[g, :, lanes]))
            if g == 1:
                dsilu_one[:, lanes] = s + act * (1.0 - s)
            total = jnp.concatenate([act[0:32] + act[32:64], act[64:96] + act[96:128]], axis=0)
            high = total.astype(BF16)
            low = (total - high.astype(F32)).astype(BF16)
            part = dot(jnp.concatenate([high, low], axis=0), pool[lanes, :])
            sums = part if sums is None else sums + part
        pooled = (sums[0:64] + sums[64:128]) * 0.125
        if g == 0:
            pooled = jnp.where(first, 0.0, pooled)
        if g == 2:
            pooled = jnp.where(last, 0.0, pooled)
        pooled = pooled.astype(BF16)
        for v in range(9):
            block = shifted_bf16(pooled, v, ones_two[v], 16)
            if g == 0:
                xcol_c[v * 128:v * 128 + 32, :] = block[32:64]
            if g == 1:
                xcol_c[v * 128 + 32:v * 128 + 96, :] = block
            if g == 2:
                xcol_c[v * 128 + 96:v * 128 + 128, :] = block[0:32]
            if g < 2:
                xcol_a[v * 128 + g * 64:v * 128 + g * 64 + 64, :] = block
            if g > 0:
                xcol_b[v * 128 + g * 64 - 64:v * 128 + g * 64, :] = block

    pl.semaphore_wait(news.at[1], len(wide))
    halos[4].wait_recv()
    halos[5].wait_recv()
    cot_a = jnp.concatenate([cotr[0].astype(F32), cots[0].astype(F32)], axis=0)
    cot_b = jnp.concatenate([cots[1].astype(F32), cotr[1].astype(F32)], axis=0)
    act_a, s_a = silu_parts(dot(w2band[...], xcol_a[...]))
    delta_a = cot_a * (s_a + act_a * (1.0 - s_a))
    act_b, s_b = silu_parts(dot(w2band[...], xcol_b[...]))
    delta_b = cot_b * (s_b + act_b * (1.0 - s_b))
    delta = jnp.concatenate(
        [
            jnp.where(first, 0.0, delta_a[0:64]),
            delta_a[64:128],
            delta_b[0:64],
            jnp.where(last, 0.0, delta_b[64:128]),
        ],
        axis=0,
    ).astype(BF16)

    rows_xy, rows_z = 64 // tiles_n, 64 // slabs
    scale_two = 1.0 / 512.0 * math.sqrt(64 * 8 / (slabs * dp_n))
    outer = dot_nt(delta[64:192], xcol_c[...])
    tiles = []
    for v in range(9):
        lanes = slice(v * 128, (v + 1) * 128)
        tiles.append(outer[0:64, lanes] + pltpu.roll(outer[64:128, lanes], 96, 1))
    lane = iota((1, 128), 1)
    for v in range(7):
        tile = tiles[v]
        if v < 6:
            kd = v % 3
            tile = jnp.where(lane < 96, tile, pltpu.roll(tiles[7 + v // 3], 96 - kd * 32, 1))
        g2s[:, :, v * 128:(v + 1) * 128] = (tile * scale_two).astype(BF16).reshape(tiles_n, rows_xy, 128)
    for r in range(1, tiles_n):
        other, peer = xy_peer(r)
        send(g2s.at[other], g2x.at[xy], xs.at[0], xr.at[0], peer)
    z = dot(wp[...], delta)
    total = None
    for v in range(9):
        term = shifted(z[v * 64:(v + 1) * 64], v, masks, 16, sign=-1)
        total = term if total is None else total + term
    pg = total.astype(BF16)

    for copy in halos:
        copy.wait_send()

    g1k = None
    for n in range(4):
        lanes = slice(n * 256, (n + 1) * 256)
        spread = dot_nt(pg, pool[lanes, :]) * 0.125
        twice = jnp.concatenate([spread[0:32], spread[0:32], spread[32:64], spread[32:64]], axis=0)
        one = (twice * dsilu_one[:, lanes]).astype(BF16)
        part = dot_nt(one, x1[1, :, lanes])
        g1k = part if g1k is None else g1k + part
    hi = g1k.astype(BF16)
    mid = (g1k - hi.astype(F32)).astype(BF16)
    g1 = None
    for d in range(4):
        rows = slice(d * 32, (d + 1) * 32)
        out = dot_nt(jnp.concatenate([hi[rows], mid[rows]], axis=0), tsel[d])
        g1 = out if g1 is None else g1 + out
    g1 = (g1[0:32] + g1[32:64]) * (1.0 / math.sqrt(4096 * slabs * dp_n))
    q_y = 32 // tiles_n
    g1s[...] = g1.reshape(tiles_n, q_y, 128)
    for r in range(1, tiles_n):
        other, peer = xy_peer(r)
        send(g1s.at[other], g1x.at[xy], xs.at[1], xr.at[1], peer)
    g2x[xy] = g2s[xy]
    g1x[xy] = g1s[xy]

    own_feat = jnp.concatenate([act_a[64:128], act_b[0:64]], axis=0).astype(BF16)
    feat[...] = dot(merge, own_feat).astype(BF16).reshape(64, 2, 256)
    pgrad[...] = dot(merge_half, pg).astype(BF16).reshape(32, 2, 256)

    f = iota((1, 896), 1)
    f_v, f_kd, f_c = f % 9, (f % 27) // 9, f // 27
    f_row = jnp.where(f_v < 7, f_v, (f_v - 7) * 3 + f_kd)
    f_lane = jnp.where(f < 864, jnp.where(f_v < 7, f_kd * 32 + f_c, 96 + f_c), -1)
    place[...] = jnp.where(iota((128, 896), 0) == f_lane, 1.0, 0.0).astype(BF16)

    def whole(src, dst, count, ssem, rsem):
        return pltpu.make_async_remote_copy(
            src_ref=src.at[0:count], dst_ref=dst.at[0:count], send_sem=ssem, recv_sem=rsem,
            device_id=at(1, 0, 0, 0), device_id_type=pl.DeviceIdType.MESH,
        )

    def fold(parts, rows):
        step = parts.shape[0]
        while step > max(rows, 8):
            step //= 2
            parts = parts[0:step] + parts[step:2 * step]
        total = parts[0:rows]
        for i in range(1, step // rows):
            total = total + parts[i * rows:(i + 1) * rows]
        return total

    all_two = whole(g2s, g2x, tiles_n - 1, xs.at[0], xr.at[0])
    all_one = whole(g1s, g1x, tiles_n - 1, xs.at[1], xr.at[1])
    all_two.wait_recv()
    sum_two = fold(g2x[...].reshape(64, cols).astype(F32), rows_xy)
    all_one.wait_recv()
    sum_one = fold(g1x[...].reshape(32, 128), q_y)
    for i in range(nz):
        rows = []
        for q in range(rows_z):
            at_row = slice(i * rows_z + q, i * rows_z + q + 1)
            rows += [sum_two[at_row, v * 128:(v + 1) * 128] for v in range(7)] + [sum_one[q:q + 1]]
        gz[i] = jnp.concatenate(rows, axis=0).astype(BF16)
    for r in range(1, team):
        other, oz, peer = z_peer(r)
        send(gz.at[oz], gr.at[me_z], zs.at[0], zr.at[0], peer)
    gr[me_z] = gz[zl]
    all_two.wait_send()
    all_one.wait_send()
    pltpu.make_async_remote_copy(
        src_ref=gr.at[0:team - 1], dst_ref=gr.at[0:team - 1], send_sem=zs.at[0], recv_sem=zr.at[0],
        device_id=at(1, 0, 0, 0), device_id_type=pl.DeviceIdType.MESH,
    ).wait()
    total = gr[0].astype(F32)
    for r in range(1, team):
        total = total + gr[r].astype(F32)
    for q in range(rows_z):
        packed = total[q * 8:q * 8 + 8]
        hi = packed.astype(BF16)
        rest = packed - hi.astype(F32)
        mid = rest.astype(BF16)
        low = (rest - mid.astype(F32)).astype(BF16)
        split3 = jnp.concatenate([hi.astype(F32), mid.astype(F32), low.astype(F32)], axis=0)
        spread = dot(split3.astype(BF16), place[...])
        spread = spread[0:8] + (spread[8:16] + spread[16:24])
        spread = jnp.where(iota((8, 896), 0) == f_row, spread, 0.0)
        g2_out[q:q + 1, :] = jnp.sum(spread, axis=0, keepdims=True)
        one = packed[7:8]
        if rows_z == 1:
            one = jnp.where(zl == 0, one, pltpu.roll(one, 128 - 54, 1))
        g1_out[q:q + 1, :] = one


def finish(feat, pgrad, g1, g2, feat_out, pgrad_out, g1_out, g2_out, one, two, sems):
    copies = [
        pltpu.make_async_copy(feat, feat_out, sems.at[0]),
        pltpu.make_async_copy(pgrad, pgrad_out, sems.at[1]),
    ]
    for copy in copies:
        copy.start()
    one[...] = g1[0, 0:54]
    two[...] = g2[0, 0:864]
    tails = [
        pltpu.make_async_copy(one, g1_out, sems.at[2]),
        pltpu.make_async_copy(two, g2_out, sems.at[3]),
    ]
    for copy in tails:
        copy.start()
    for copy in copies + tails:
        copy.wait()


def on_device(sizes, volumes, kernel_one, kernel_two, cotangent):
    nx, ny, nz, dp_n = sizes
    slabs, team = nx * ny * nz, nz * dp_n
    w1 = jnp.transpose(kernel_one, (2, 3, 4, 1, 0)).reshape(27, 4, 32)
    w2 = jnp.transpose(kernel_two, (2, 3, 4, 1, 0)).reshape(27, 32, 64)
    tiles_n = nx * ny
    rows_xy, rows_z, q_y = 64 // tiles_n, 64 // slabs, 32 // tiles_n
    cols = 896
    vmem = pl.BlockSpec(memory_space=pltpu.VMEM)
    hbm = pl.BlockSpec(memory_space=pltpu.HBM)
    scratch = [
        ((4, 4, 32, 32), BF16),
        ((27, 4, 32), BF16),
        ((27, 32, 64), BF16),
        ((64, 2, 256), BF16),
        ((512, 32), F32),
        ((16, 4, 1024), BF16),
        ((2, 64, 256), BF16),
        ((2, 64, 256), BF16),
        ((128, 128), F32),
        ((9, 16, 1024), BF16),
        ((9, 16, 256), BF16),
        ((3, 224, 1024), BF16),
        ((4, 128, 224), BF16),
        ((128, 224), BF16),
        ((1024, 256), BF16),
        ((128, 1024), F32),
        ((128, 1152), BF16),
        ((576, 256), BF16),
        ((128, cols), BF16),
        ((1152, 256), BF16),
        ((1152, 256), BF16),
        ((1152, 256), BF16),
        ((tiles_n, rows_xy, cols), BF16),
        ((tiles_n, rows_xy, cols), BF16),
        ((tiles_n, q_y, 128), F32),
        ((tiles_n, q_y, 128), F32),
        ((nz, rows_z * 8, 128), BF16),
        ((team, rows_z * 8, 128), BF16),
    ]
    dma = pltpu.SemaphoreType.DMA
    features, pooled_grad, g1, g2 = pl.pallas_call(
        functools.partial(kernel, sizes, cols),
        out_shape=(
            jax.ShapeDtypeStruct((64, 2, 256), BF16),
            jax.ShapeDtypeStruct((32, 2, 256), BF16),
            jax.ShapeDtypeStruct((q_y, 128), F32),
            jax.ShapeDtypeStruct((rows_z, cols), F32),
        ),
        in_specs=[hbm] * 4,
        out_specs=(vmem,) * 4,
        scratch_shapes=[pltpu.VMEM(shape, dtype) for shape, dtype in scratch] + [
            dma((4,)), dma((6,)), dma((6,)),
            dma((2,)), dma((2,)), dma((1,)), dma((1,)),
            pltpu.SemaphoreType.REGULAR((2,)),
        ],
        compiler_params=pltpu.CompilerParams(
            collective_id=0, has_side_effects=True, vmem_limit_bytes=24 * 2**20
        ),
        name="conv_step",
    )(*(pltpu.with_memory_space_constraint(a, pltpu.HBM) for a in (volumes[0], w1, w2, cotangent[0])))
    if q_y > 1:
        half = q_y * 108 // nz
        zl = lax.rem(lax.axis_index("space"), nz)
        grad_one = lax.dynamic_slice_in_dim(g1[:, :108].reshape(-1), zl * half, half, 0)
        return features[None], pooled_grad[None], grad_one, g2[:, :864].reshape(-1)
    features, pooled_grad, grad_one, grad_two = pl.pallas_call(
        finish,
        out_shape=(
            jax.ShapeDtypeStruct((64, 2, 256), BF16),
            jax.ShapeDtypeStruct((32, 2, 256), BF16),
            jax.ShapeDtypeStruct((54,), F32),
            jax.ShapeDtypeStruct((864,), F32),
        ),
        in_specs=[vmem] * 4,
        out_specs=(hbm,) * 4,
        scratch_shapes=[pltpu.VMEM((54,), F32), pltpu.VMEM((864,), F32), dma((4,))],
        compiler_params=pltpu.CompilerParams(vmem_limit_bytes=2 * 2**20),
        name="finish",
    )(features, pooled_grad, g1, g2)
    return features[None], pooled_grad[None], grad_one, grad_two


def solution(mesh):
    slabs, dp_n = mesh.shape["space"], mesh.shape["dp"]
    sizes = (4, 8, 2, dp_n) if slabs == 64 else (2, 2, slabs // 4, dp_n)
    in_specs = (P("dp", None, "space", None, None), P(), P(), P("dp", None, "space", None))
    out_specs = (P("dp", None, "space", None), P("dp", None, "space", None), P("space"), P("space"))
    return jax.shard_map(
        functools.partial(on_device, sizes), mesh=mesh, in_specs=in_specs, out_specs=out_specs,
        check_vma=False,
    )
```
